128 devices in a mesh: row: 8 (over x_lo, z), col: 16 (over x_hi, y, core).
Axes of the slice: x: 4 (x_hi: 2, x_lo: 2; x = x_hi * 2 + x_lo), y: 4, z: 4, core: 2. Of those that a mesh axis runs over, the one named last changes fastest.
Arguments:
- ancestor: float32 [24576, 24576], P('row', 'col'), may hold values from -6 to 6
- lhat_one: float32 [24576, 512], P('col', 'row'), may hold values from -0.15625 to 0.15625
- lhat_two: float32 [24576, 512], P('col', 'row'), may hold values from -0.15625 to 0.15625
- link_two: float32 [512, 512], replicated, may hold values from -0.25 to 0.25
- diag_one: float32 [512, 512], replicated, may hold values from -6 to 6
- diag_two: float32 [512, 512], replicated, may hold values from -6 to 6
- mask_one: int32 [192], replicated, may hold values from 0 to 1, as said below
- mask_two: int32 [192], replicated, may hold values from 0 to 1, as said below
Outputs:
- x_one: float32 [24576, 512], P('row', 'col')
- d_one: float32 [512, 512], replicated
- x_two: float32 [24576, 512], P('row', 'col')
- link_inverse: float32 [512, 512], replicated
- d_two: float32 [512, 512], replicated
The draws below stay inside these ranges and needn't reach their ends.
Inputs may be any that keep to these rules, and one draw needn't show every extreme that they name: `mask_one`: 1 where a block of 128 factor rows is nonzero, else 0; the last block is always nonzero. `mask_two`: 1 where a block of 128 factor rows is nonzero, else 0; the last block is always nonzero.
All inputs are finite; a program needn't handle non-finite values.
Results may differ from the reference program's by a relative error of at most 0.00011.
Values sent between devices are 32-bit elements; how exact they have to be, the bound alone decides.
No kernel may reach another device: no remote copies, remote signals or barrier semaphores. Data moves between devices by JAX's collectives and lax.ppermute only.
A program may use at most 128 MiB of HBM per device.

```python
import jax
import jax.numpy as jnp
from jax import lax

NA = 24576
W = 512
BLOCK = 128
NB = 192
N_COL = 16


def skewed_mask(key):
    position = jnp.arange(NB, dtype=jnp.int32)
    threshold = 150 + 850 * position // max(NB - 1, 1)
    drawn = jax.random.randint(key, (NB,), 0, 1000, dtype=jnp.int32)
    return (drawn < threshold).astype(jnp.int32)


def draw_mask_one(key, part):
    return skewed_mask(jax.random.fold_in(key, 11))


def draw_mask_two(key, part):
    return skewed_mask(jax.random.fold_in(key, 23))


def steps_of(stream_key, dims, split, least, top_value):
    level, own = 1.0, jax.random.fold_in(stream_key, 6)
    for dim, parts in split:
        steps = jnp.exp(jax.random.uniform(jax.random.fold_in(own, dim), (parts,), jnp.float32, least / len(split), top_value / len(split)))
        level = level * jnp.repeat(steps, dims[dim] // parts).reshape([-1 if axis == dim else 1 for axis in range(len(dims))])
    return level


def gaussian(own_key, extent, deviation, limit, split=(), kind=jnp.bfloat16):
    array = jax.random.normal(own_key, extent, jnp.float32) * deviation
    if len(split) > 0:
        array = steps_of(own_key, extent, split, -0.22, 0.18) * array
    return jnp.clip(array, min=-limit, max=limit).astype(kind)


def setup_inputs(seed: int = 0) -> dict:
    key_list = jax.random.split(jax.random.key(seed), 9)
    ancestor = gaussian(key_list[0], (NA, NA), 1.0, 6.0, ((0, 8), (1, 16)), jnp.float32)
    lhat_one = gaussian(key_list[1], (NA, W), (NA // N_COL) ** -0.5, 0.15625, ((0, 16), (1, 8)), jnp.float32)
    lhat_two = gaussian(key_list[2], (NA, W), (NA // N_COL) ** -0.5, 0.15625, ((0, 16), (1, 8)), jnp.float32)
    link_two = gaussian(key_list[3], (W, W), W ** -0.5, 0.25, (), jnp.float32)
    diag_one = gaussian(key_list[4], (W, W), 1.0, 6.0, (), jnp.float32)
    diag_two = gaussian(key_list[5], (W, W), 1.0, 6.0, (), jnp.float32)
    mask_one = draw_mask_one(jax.random.fold_in(key_list[8], 71), 0)
    mask_two = draw_mask_two(jax.random.fold_in(key_list[8], 71), 0)
    return dict(ancestor=ancestor, lhat_one=lhat_one, lhat_two=lhat_two, link_two=link_two, diag_one=diag_one, diag_two=diag_two, mask_one=mask_one, mask_two=mask_two)


def masked(factor_rows, block_mask):
    expanded = jnp.repeat(block_mask.astype(jnp.float32), BLOCK, total_repeat_length=NA)
    return factor_rows * expanded[:, None]


def product(left, right):
    return jnp.dot(left, right, precision=lax.Precision.HIGHEST, preferred_element_type=jnp.float32)


def reference(ancestor, lhat_one, lhat_two, link_two, diag_one, diag_two, mask_one, mask_two):
    factor_one = masked(lhat_one, mask_one)
    factor_two = masked(lhat_two, mask_two)
    x_one = -product(ancestor, factor_one)
    d_one = diag_one - product(factor_one.T, x_one)
    x_two = -(product(ancestor, factor_two) + product(x_one, link_two))
    link_inverse = -(product(x_one.T, factor_two) + product(d_one, link_two))
    d_two = diag_two - product(factor_two.T, x_two) - product(link_two.T, link_inverse)
    return x_one, d_one, x_two, link_inverse, d_two
```

```python
import jax
import jax.numpy as jnp
from jax import lax
from jax.sharding import Mesh, PartitionSpec as P

BLOCK = 128
ROW = ("xl", "z")
COL = ("xh", "y", "core")
ALL = ROW + COL
SIZES = (2, 4, 2, 4, 2)
SWAP = ((0, 1), (1, 0))


def product(left, right, contract=((1,), (0,))):
    return lax.dot_general(left, right, (contract, ((), ())), precision=lax.Precision.HIGH,
                           preferred_element_type=jnp.float32)


def linear(xl, z, xh, y, core):
    return (((xl * 4 + z) * 2 + xh) * 4 + y) * 2 + core


def factor_routes():
    routes = []
    for xl in range(2):
        for z in range(4):
            for xh in range(2):
                for y in range(4):
                    for core in range(2):
                        source = linear(y // 2, (y % 2) * 2 + core, xl, z, xh)
                        routes.append((source, linear(xl, z, xh, y, core)))
    return routes


def per_device(ancestor, lhat_one, lhat_two, link_two, diag_one, diag_two, mask_one, mask_two):
    row_index = lax.axis_index(ROW)
    column_index = lax.axis_index(COL)
    core = lax.axis_index("core")
    xh = lax.axis_index("xh")
    rows, depth = ancestor.shape
    width = link_two.shape[0]
    blocks = depth // BLOCK
    part = rows // 16

    def masked(shard, mask):
        own = lax.dynamic_slice_in_dim(mask, column_index * blocks, blocks).astype(jnp.float32)
        return (shard.reshape(blocks, BLOCK, -1) * own[:, None, None]).reshape(shard.shape)

    def row_sum(factor):
        partial = product(ancestor, factor).reshape(2, 4, 2, part, width)
        keep = lax.dynamic_index_in_dim(partial, core, 2, keepdims=False)
        send = lax.dynamic_index_in_dim(partial, 1 - core, 2, keepdims=False)
        chip = keep + lax.ppermute(send, "core", SWAP)
        chip = chip.transpose(1, 0, 2, 3).reshape(8 * part, width)
        line = lax.psum_scatter(chip, "y", scatter_dimension=0, tiled=True).reshape(2, part, width)
        own = lax.dynamic_index_in_dim(line, xh, 0, keepdims=False)
        other = lax.dynamic_index_in_dim(line, 1 - xh, 0, keepdims=False)
        return own + lax.ppermute(other, "xh", SWAP)

    factor_one = lax.all_gather(masked(lhat_one, mask_one), ROW, axis=1, tiled=True)
    factor_two = lax.all_gather(masked(lhat_two, mask_two), ROW, axis=1, tiled=True)
    local = jnp.concatenate(
        [lax.dynamic_slice_in_dim(f, row_index * part, part, 0) for f in (factor_one, factor_two)], axis=1)
    local = lax.ppermute(local, ALL, factor_routes())
    sum_one = row_sum(factor_one)
    sum_two = row_sum(factor_two)
    gram_one = product(local, sum_one, ((0,), (0,)))
    gram_two = product(local[:, width:], sum_two, ((0,), (0,)))
    grams = jnp.concatenate([gram_one, gram_two], axis=0)
    half = grams.shape[0] // 2
    keep = lax.dynamic_slice_in_dim(grams, core * half, half, 0)
    send = lax.dynamic_slice_in_dim(grams, (1 - core) * half, half, 0)
    piece = keep + lax.ppermute(send, "core", SWAP)
    piece = lax.psum_scatter(piece, "y", scatter_dimension=0, tiled=True)
    piece = lax.psum_scatter(piece, "z", scatter_dimension=0, tiled=True)
    piece = lax.psum(piece, ("xl", "xh"))
    piece = lax.all_gather(piece, "z", axis=0, tiled=True)
    piece = lax.all_gather(piece, "y", axis=0, tiled=True)
    other = lax.ppermute(piece, "core", SWAP)
    grams = jnp.where(core == 0, jnp.concatenate([piece, other], 0), jnp.concatenate([other, piece], 0))
    cross = grams[width:2 * width]
    d_one = diag_one + grams[:width]
    link_inverse = cross.T - product(d_one, link_two)
    d_two = diag_two + grams[2 * width:] - product(cross, link_two) - product(link_two, link_inverse, ((0,), (0,)))
    own_two = product(sum_one, link_two) - sum_two
    out = jnp.stack([-sum_one, own_two], axis=0)
    out = lax.all_to_all(out, COL, split_axis=2, concat_axis=1, tiled=True)
    return (out[0], d_one, out[1], link_inverse, d_two)


def solution(mesh):
    fine = Mesh(mesh.devices.reshape(SIZES), ALL)
    in_specs = (P(ROW, COL), P(COL, ROW), P(COL, ROW), P(), P(), P(), P(), P())
    out_specs = (P(ROW, COL), P(), P(ROW, COL), P(), P())
    return jax.shard_map(
        per_device, mesh=fine, in_specs=in_specs, out_specs=out_specs, check_vma=False
    )
```

```python
import jax
import jax.numpy as jnp
from jax import lax
from jax.experimental import pallas as pl
from jax.experimental.pallas import tpu as pltpu
from jax.sharding import Mesh, PartitionSpec as P

BLOCK = 128
ROW = ("xl", "z")
COL = ("xh", "y", "core")
PLANE = ("xh", "y")
CHIPS = ("xl", "z", "xh", "y")
ALL = ROW + COL
SIZES = (2, 4, 2, 4, 2)
SWAP = ((0, 1), (1, 0))
TILES = 2


def product(left, right, contract=((1,), (0,))):
    return lax.dot_general(left, right, (contract, ((), ())), precision=lax.Precision.HIGH,
                           preferred_element_type=jnp.float32)


def linear(xl, z, xh, y, core):
    return (((xl * 4 + z) * 2 + xh) * 4 + y) * 2 + core


def factor_routes():
    routes = []
    for xl in range(2):
        for z in range(4):
            for xh in range(2):
                for y in range(4):
                    for core in range(2):
                        source = linear(y // 2, (y % 2) * 2 + core, xl, z, xh)
                        routes.append((source, linear(xl, z, xh, y, core)))
    return routes


def split(value):
    high = value.astype(jnp.bfloat16)
    return high, (value - high.astype(jnp.float32)).astype(jnp.bfloat16)


def half_kernel(side_ref, a_ref, factor_ref, after_ref, out_ref, high_ref, low_ref):
    del side_ref, after_ref

    @pl.when(pl.program_id(0) == 0)
    def _():
        high, low = split(factor_ref[...])
        high_ref[...] = high
        low_ref[...] = low

    tiles, part, depth = a_ref.shape
    a_high, a_low = split(a_ref[...].reshape(tiles * part, depth))
    dims = (((1,), (1,)), ((), ()))
    dot = lambda l, r: lax.dot_general(l, r, dims, preferred_element_type=jnp.float32)
    total = dot(a_high, high_ref[...]) + dot(a_high, low_ref[...]) + dot(a_low, high_ref[...])
    out_ref[...] = total.reshape(out_ref.shape)


def half_product(ancestor, factor_t, side, after):
    rows, depth = ancestor.shape
    width = factor_t.shape[0]
    part = rows // 16
    view = ancestor.reshape(8, 2, part, depth)
    return pl.pallas_call(
        half_kernel,
        grid_spec=pltpu.PrefetchScalarGridSpec(
            num_scalar_prefetch=1,
            grid=(8 // TILES,),
            in_specs=[
                pl.BlockSpec((TILES, None, part, depth), lambda i, side: (i, side[0], 0, 0)),
                pl.BlockSpec((width, depth), lambda i, side: (0, 0), pipeline_mode=pl.Buffered(1)),
                pl.BlockSpec(memory_space=pl.ANY),
            ],
            out_specs=pl.BlockSpec((TILES, part, width), lambda i, side: (i, 0, 0)),
            scratch_shapes=[pltpu.VMEM((width, depth), jnp.bfloat16)] * 2,
        ),
        out_shape=jax.ShapeDtypeStruct((8, part, width), jnp.float32),
        cost_estimate=pl.CostEstimate(
            flops=3 * rows * depth * width, transcendentals=0,
            bytes_accessed=2 * rows * depth + 4 * width * depth + 2 * rows * width),
        compiler_params=pltpu.CompilerParams(vmem_limit_bytes=40 * 1024 * 1024),
    )(side.reshape(1), view, factor_t, after)


def per_device(ancestor, lhat_one, lhat_two, link_two, diag_one, diag_two, mask_one, mask_two):
    row_index = lax.axis_index(ROW)
    column_index = lax.axis_index(COL)
    core = lax.axis_index("core")
    rows, depth = ancestor.shape
    width = link_two.shape[0]
    blocks = depth // BLOCK
    part = rows // 16
    half = width // 2

    def masked(shard, mask):
        own = lax.dynamic_slice_in_dim(mask, column_index * blocks, blocks).astype(jnp.float32)
        return shard.T * jnp.broadcast_to(own[:, None], (blocks, BLOCK)).reshape(1, depth)

    def row_sum(factor_t, after):
        send = half_product(ancestor, factor_t, 1 - core, after)
        keep = half_product(ancestor, factor_t, core, send)
        chip = keep + lax.ppermute(send, "core", SWAP)
        pieces = lax.all_to_all(chip, PLANE, split_axis=0, concat_axis=0, tiled=True)
        return pieces.sum(0), keep

    def to_columns(own_rows):
        pieces = lax.all_to_all(own_rows.T, COL, split_axis=0, concat_axis=0, tiled=True)
        return pieces.reshape(16, width // 16, part).transpose(0, 2, 1).reshape(rows, width // 16)

    def half_of(value, side):
        return lax.dynamic_slice_in_dim(value, side * half, half, 0)

    factor_one = lax.all_gather(masked(lhat_one, mask_one), ROW, axis=0, tiled=True)
    factor_two = lax.all_gather(masked(lhat_two, mask_two), ROW, axis=0, tiled=True)
    local = jnp.concatenate(
        [lax.dynamic_slice_in_dim(f, row_index * part, part, 1) for f in (factor_one, factor_two)], axis=0)
    local = lax.ppermute(local, ALL, factor_routes())
    sum_one, done_one = row_sum(factor_one, link_two)
    one_part = product(local[:width], sum_one)
    link_part = product(sum_one, local[width:], ((0,), (1,))) - product(one_part, link_two)
    moved_one = product(sum_one, link_two)
    last_part = product(link_two, link_part, ((0,), (0,))) + product(local[width:], moved_one)
    sum_two, _ = row_sum(factor_two, done_one)
    x_one, sum_two = lax.optimization_barrier((to_columns(-sum_one), sum_two))
    two_part = product(local[width:], sum_two) - last_part
    link_base = -product(diag_one, link_two)
    two_base = diag_two - product(link_two, link_base, ((0,), (0,)))
    parts = (one_part, link_part, two_part)
    keep = jnp.concatenate([half_of(p, core) for p in parts])
    send = jnp.concatenate([half_of(p, 1 - core) for p in parts])
    chip = keep + lax.ppermute(send, "core", SWAP)
    chips = 64
    piece = lax.all_to_all(chip.reshape(chips, 3 * half // chips, width), CHIPS,
                           split_axis=0, concat_axis=0, tiled=True).sum(0)
    whole = lax.all_to_all(jnp.broadcast_to(piece[None], (chips,) + piece.shape), CHIPS,
                           split_axis=0, concat_axis=0, tiled=True).reshape(3 * half, width)
    other = lax.ppermute(whole, "core", SWAP)
    low = jnp.where(core == 0, whole, other)
    high = jnp.where(core == 0, other, whole)

    def joined(index, base):
        cut = slice(index * half, (index + 1) * half)
        return jnp.concatenate([low[cut], high[cut]]) + base

    return (x_one, joined(0, diag_one), to_columns(moved_one - sum_two),
            joined(1, link_base), joined(2, two_base))


def solution(mesh):
    fine = Mesh(mesh.devices.reshape(SIZES), ALL)
    in_specs = (P(ROW, COL), P(COL, ROW), P(COL, ROW), P(), P(), P(), P(), P())
    out_specs = (P(ROW, COL), P(), P(ROW, COL), P(), P())
    return jax.shard_map(
        per_device, mesh=fine, in_specs=in_specs, out_specs=out_specs, check_vma=False
    )
```

```python
import jax
import jax.numpy as jnp
from jax import lax
from jax.experimental import pallas as pl
from jax.experimental.pallas import tpu as pltpu
from jax.sharding import Mesh, PartitionSpec as P


BLOCK = 128
ROW = ("xl", "z")
COL = ("xh", "y", "core")
PLANE = ("xh", "y")
CHIPS = ("xl", "z", "xh", "y")
ALL = ROW + COL
SIZES = (2, 4, 2, 4, 2)
SWAP = ((0, 1), (1, 0))
TILES = 2


def product(left, right, contract=((1,), (0,))):
    return lax.dot_general(left, right, (contract, ((), ())), precision=lax.Precision.HIGH,
                           preferred_element_type=jnp.float32)


def linear(xl, z, xh, y, core):
    return (((xl * 4 + z) * 2 + xh) * 4 + y) * 2 + core


def factor_routes():
    routes = []
    for xl in range(2):
        for z in range(4):
            for xh in range(2):
                for y in range(4):
                    for core in range(2):
                        source = linear(y // 2, (y % 2) * 2 + core, xl, z, xh)
                        routes.append((source, linear(xl, z, xh, y, core)))
    return routes


def split(value):
    high = value.astype(jnp.bfloat16)
    return high, (value - high.astype(jnp.float32)).astype(jnp.bfloat16)


def half_kernel(side_ref, a_ref, factor_ref, after_ref, out_ref, high_ref, low_ref):
    del side_ref, after_ref

    @pl.when(pl.program_id(0) == 0)
    def _():
        high, low = split(factor_ref[...])
        high_ref[...] = high
        low_ref[...] = low

    tiles, part, depth = a_ref.shape
    a_high, a_low = split(a_ref[...].reshape(tiles * part, depth))
    dims = (((1,), (1,)), ((), ()))
    dot = lambda l, r: lax.dot_general(l, r, dims, preferred_element_type=jnp.float32)
    total = dot(a_high, high_ref[...]) + dot(a_high, low_ref[...]) + dot(a_low, high_ref[...])
    out_ref[...] = total.reshape(out_ref.shape)


def half_product(ancestor, factor_t, side, after):
    rows, depth = ancestor.shape
    width = factor_t.shape[0]
    part = rows // 16
    view = ancestor.reshape(8, 2, part, depth)
    return pl.pallas_call(
        half_kernel,
        grid_spec=pltpu.PrefetchScalarGridSpec(
            num_scalar_prefetch=1,
            grid=(8 // TILES,),
            in_specs=[
                pl.BlockSpec((TILES, None, part, depth), lambda i, side: (i, side[0], 0, 0)),
                pl.BlockSpec((width, depth), lambda i, side: (0, 0), pipeline_mode=pl.Buffered(1)),
                pl.BlockSpec(memory_space=pl.ANY),
            ],
            out_specs=pl.BlockSpec((TILES, part, width), lambda i, side: (i, 0, 0)),
            scratch_shapes=[pltpu.VMEM((width, depth), jnp.bfloat16)] * 2,
        ),
        out_shape=jax.ShapeDtypeStruct((8, part, width), jnp.float32),
        cost_estimate=pl.CostEstimate(
            flops=3 * rows * depth * width, transcendentals=0,
            bytes_accessed=2 * rows * depth + 4 * width * depth + 2 * rows * width),
        compiler_params=pltpu.CompilerParams(vmem_limit_bytes=40 * 1024 * 1024),
    )(side.reshape(1), view, factor_t, after)


def per_device(ancestor, lhat_one, lhat_two, link_two, diag_one, diag_two, mask_one, mask_two):
    row_index = lax.axis_index(ROW)
    column_index = lax.axis_index(COL)
    core = lax.axis_index("core")
    rows, depth = ancestor.shape
    width = link_two.shape[0]
    blocks = depth // BLOCK
    part = rows // 16
    half = width // 2

    def masked(shard, mask):
        own = lax.dynamic_slice_in_dim(mask, column_index * blocks, blocks).astype(jnp.float32)
        return shard.T * jnp.broadcast_to(own[:, None], (blocks, BLOCK)).reshape(1, depth)

    def row_sum(factor_t, after):
        send = half_product(ancestor, factor_t, 1 - core, after)
        received = lax.ppermute(send, "core", SWAP)
        keep = half_product(ancestor, factor_t, core, send)
        chip = keep + received
        pieces = lax.all_to_all(chip, PLANE, split_axis=0, concat_axis=0, tiled=True)
        return pieces.sum(0), keep

    def to_columns(own_rows):
        own_rows = jnp.concatenate([value.T for value in own_rows], axis=1)
        pieces = lax.all_to_all(own_rows, COL, split_axis=0, concat_axis=0, tiled=True)
        pieces = pieces.reshape(16, width // 16, 2, part).transpose(2, 0, 3, 1)
        return pieces.reshape(2, rows, width // 16)

    def half_of(value, side):
        return lax.dynamic_slice_in_dim(value, side * half, half, 0)

    def gathered(shard, mask):
        shard = masked(shard, mask)
        full = lax.all_gather(shard, ROW, axis=0, tiled=True)
        rows_here = lax.dynamic_slice_in_dim(full, row_index * part, part, 1)
        local = lax.ppermute(rows_here, ALL, factor_routes())
        return full, local

    factor_one, local_one = gathered(lhat_one, mask_one)
    factor_two, local_two = gathered(lhat_two, mask_two)
    sum_one, done_one = row_sum(factor_one, link_two)
    sum_two, _ = row_sum(factor_two, done_one)
    one_part = product(local_one, sum_one)
    link_part = product(sum_one, local_two, ((0,), (1,))) - product(one_part, link_two)
    moved_one = product(sum_one, link_two)
    last_part = product(link_two, link_part, ((0,), (0,))) + product(local_two, moved_one)
    two_part = product(local_two, sum_two) - last_part
    link_base = -product(diag_one, link_two)
    two_base = diag_two - product(link_two, link_base, ((0,), (0,)))
    link_base, two_base = lax.optimization_barrier((link_base, two_base))
    parts = (one_part, link_part, two_part)
    keep = jnp.concatenate([half_of(p, core) for p in parts])
    send = jnp.concatenate([half_of(p, 1 - core) for p in parts])
    chip = keep + lax.ppermute(send, "core", SWAP)
    chips = 64
    piece = lax.all_to_all(chip.reshape(chips, 3 * half // chips, width), CHIPS,
                           split_axis=0, concat_axis=0, tiled=True).sum(0)
    whole = lax.all_to_all(jnp.broadcast_to(piece[None], (chips,) + piece.shape), CHIPS,
                           split_axis=0, concat_axis=0, tiled=True).reshape(3 * half, width)
    other = lax.ppermute(whole, "core", SWAP)
    low = jnp.where(core == 0, whole, other)
    high = jnp.where(core == 0, other, whole)

    def joined(index, base):
        cut = slice(index * half, (index + 1) * half)
        return jnp.concatenate([low[cut], high[cut]]) + base

    x_one, x_two = to_columns((-sum_one, moved_one - sum_two))
    return (x_one, joined(0, diag_one), x_two, joined(1, link_base), joined(2, two_base))


def solution(mesh):
    fine = Mesh(mesh.devices.reshape(SIZES), ALL)
    in_specs = (P(ROW, COL), P(COL, ROW), P(COL, ROW), P(), P(), P(), P(), P())
    out_specs = (P(ROW, COL), P(), P(ROW, COL), P(), P())
    return jax.shard_map(
        per_device, mesh=fine, in_specs=in_specs, out_specs=out_specs, check_vma=False
    )
```

```python
import jax
import jax.numpy as jnp
from jax import lax
from jax.experimental import pallas as pl
from jax.experimental.pallas import tpu as pltpu
from jax.sharding import Mesh, PartitionSpec as P


BLOCK = 128
ROW = ("xl", "z")
COL = ("xh", "y", "core")
PLANE = ("xh", "y")
CHIPS = ("xl", "z", "xh", "y")
ALL = ROW + COL
SIZES = (2, 4, 2, 4, 2)
SWAP = ((0, 1), (1, 0))


def product(left, right, contract=((1,), (0,))):
    return lax.dot_general(left, right, (contract, ((), ())), precision=lax.Precision.HIGH,
                           preferred_element_type=jnp.float32)


def linear(xl, z, xh, y, core):
    return (((xl * 4 + z) * 2 + xh) * 4 + y) * 2 + core


def factor_routes():
    routes = []
    for xl in range(2):
        for z in range(4):
            for xh in range(2):
                for y in range(4):
                    for core in range(2):
                        source = linear(xh, (y - z) % 4, xl, z, core)
                        routes.append((source, linear(xl, z, xh, y, core)))
    return routes


def split(value):
    high = value.astype(jnp.bfloat16)
    return high, (value - high.astype(jnp.float32)).astype(jnp.bfloat16)


def multiply(a_ref, high_ref, low_ref, out_ref):
    a_high, a_low = split(a_ref[...])
    dims = (((1,), (1,)), ((), ()))
    dot = lambda l, r: lax.dot_general(l, r, dims, preferred_element_type=jnp.float32)
    out_ref[...] = dot(a_high, high_ref[...]) + dot(a_high, low_ref[...]) + dot(a_low, high_ref[...])


def first_kernel(place_ref, a_ref, *refs):
    pieces, (after_ref, out_ref, factor_ref, high_ref, low_ref) = refs[:8], refs[8:]
    del after_ref

    @pl.when(pl.program_id(0) == 0)
    def _():
        for index, piece_ref in enumerate(pieces):
            size = piece_ref.shape[0]
            span = pl.ds(pl.multiple_of(place_ref[1 + index] * size, size), size)
            value = piece_ref[...]
            high, low = split(value)
            factor_ref[span, :] = value
            high_ref[span, :] = high
            low_ref[span, :] = low

    multiply(a_ref, high_ref, low_ref, out_ref)


def second_kernel(place_ref, a_ref, factor_ref, after_ref, out_ref, high_ref, low_ref):
    del place_ref, after_ref

    @pl.when(pl.program_id(0) == 0)
    def _():
        high, low = split(factor_ref[...])
        high_ref[...] = high
        low_ref[...] = low

    multiply(a_ref, high_ref, low_ref, out_ref)


def half_product(ancestor, factors, places, after):
    rows, depth = ancestor.shape
    width = sum(f.shape[0] for f in factors)
    tile = rows // 8
    whole = pl.BlockSpec((width, depth), lambda i, places: (0, 0), pipeline_mode=pl.Buffered(1))
    piece = pl.BlockSpec((width // 8, depth), lambda i, places: (0, 0), pipeline_mode=pl.Buffered(1))
    first = len(factors) == 8
    out_shape = [jax.ShapeDtypeStruct((rows // 2, width), jnp.float32)]
    out_specs = [pl.BlockSpec((tile, width), lambda i, places: (i, 0))]
    if first:
        out_shape.append(jax.ShapeDtypeStruct((width, depth), jnp.float32))
        out_specs.append(whole)
    result = pl.pallas_call(
        first_kernel if first else second_kernel,
        grid_spec=pltpu.PrefetchScalarGridSpec(
            num_scalar_prefetch=1,
            grid=(4,),
            in_specs=[
                pl.BlockSpec((tile, depth), lambda i, places: (places[0] * 4 + i, 0)),
                *([piece] * 8 if first else [whole]),
                pl.BlockSpec(memory_space=pl.ANY),
            ],
            out_specs=out_specs,
            scratch_shapes=[pltpu.VMEM((width, depth), jnp.bfloat16)] * 2,
        ),
        out_shape=out_shape,
        cost_estimate=pl.CostEstimate(
            flops=3 * rows * depth * width, transcendentals=0,
            bytes_accessed=2 * rows * depth + 4 * width * depth + 2 * rows * width),
        compiler_params=pltpu.CompilerParams(vmem_limit_bytes=40 * 1024 * 1024),
    )(places, ancestor, *factors, after)
    return result if first else result[0]


def per_device(ancestor, lhat_one, lhat_two, link_two, diag_one, diag_two, mask_one, mask_two):
    column_index = lax.axis_index(COL)
    core = lax.axis_index("core")
    rows, depth = ancestor.shape
    width = link_two.shape[0]
    blocks = depth // BLOCK
    part = rows // 16
    half = width // 2

    xl, z = lax.axis_index("xl"), lax.axis_index("z")
    up = [(i, (i + 1) % 4) for i in range(4)]
    down = [(i, (i - 1) % 4) for i in range(4)]
    here = [xl * 4 + (z + step) % 4 for step in range(4)]
    there = [(1 - xl) * 4 + (z + step) % 4 for step in range(4)]
    places = [here[0], there[0], here[3], here[1], there[3], there[1], here[2], there[2]]
    places = {side: jnp.stack([chosen] + places).astype(jnp.int32)
              for side, chosen in (("own", core), ("other", 1 - core))}
    sub = xl * 4 + (z + lax.axis_index("y")) % 4

    def masked(shard, mask):
        own = lax.dynamic_slice_in_dim(mask, column_index * blocks, blocks).astype(jnp.float32)
        return shard.T * jnp.broadcast_to(own[:, None], (blocks, BLOCK)).reshape(1, depth)

    def gathered(piece):
        below = lax.ppermute(piece, "z", up)
        above = lax.ppermute(piece, "z", down)
        side = lax.ppermute(piece, "xl", SWAP)
        side_below = lax.ppermute(side, "z", up)
        side_above = lax.ppermute(side, "z", down)
        far = lax.ppermute(below, "z", up)
        side_far = lax.ppermute(side_above, "z", down)
        return [piece, side, below, above, side_below, side_above, far, side_far]

    def row_sum(pieces, after):
        send, factor_t = half_product(ancestor, pieces, places["other"], after)
        received = lax.ppermute(send, "core", SWAP)
        local = lax.dynamic_slice_in_dim(factor_t, sub * part, part, 1)
        local = lax.ppermute(local, ALL, factor_routes())
        keep = half_product(ancestor, [factor_t], places["own"], send)
        chip = (keep + received).reshape(8, part, width)
        pieces = lax.all_to_all(chip, PLANE, split_axis=0, concat_axis=0, tiled=True)
        return pieces.sum(0), local, send

    def to_columns(own_rows):
        own_rows = jnp.concatenate([value.T for value in own_rows], axis=1)
        pieces = lax.all_to_all(own_rows, COL, split_axis=0, concat_axis=0, tiled=True)
        pieces = pieces.reshape(8, 2, width // 16, 2 * part)
        return [pieces[..., i * part:(i + 1) * part].transpose(2, 1, 0, 3).reshape(width // 16, rows).T
                for i in range(2)]

    def half_of(value, side):
        return lax.dynamic_slice_in_dim(value, side * half, half, 0)

    piece_one = masked(lhat_one, mask_one)
    piece_two = masked(lhat_two, mask_two)
    pieces_one = gathered(piece_one)
    piece_two, *pieces_one = lax.optimization_barrier((piece_two, *pieces_one))
    pieces_two = gathered(piece_two)
    sum_one, local_one, done_one = row_sum(pieces_one, link_two)
    sum_two, local_two, _ = row_sum(pieces_two, done_one)
    one_part = product(local_one, sum_one)
    link_part = product(sum_one, local_two, ((0,), (1,))) - product(one_part, link_two)
    moved_one = product(sum_one, link_two)
    last_part = product(link_two, link_part, ((0,), (0,))) + product(local_two, moved_one)
    two_part = product(local_two, sum_two) - last_part
    link_base = -product(diag_one, link_two)
    two_base = diag_two - product(link_two, link_base, ((0,), (0,)))
    link_base, two_base = lax.optimization_barrier((link_base, two_base))
    parts = (one_part, link_part, two_part)
    keep = jnp.concatenate([half_of(p, core) for p in parts])
    send = jnp.concatenate([half_of(p, 1 - core) for p in parts])
    chip = keep + lax.ppermute(send, "core", SWAP)
    chips = 64
    piece = lax.all_to_all(chip.reshape(chips, 3 * half // chips, width), CHIPS,
                           split_axis=0, concat_axis=0, tiled=True).sum(0)
    whole = lax.all_to_all(jnp.broadcast_to(piece[None], (chips,) + piece.shape), CHIPS,
                           split_axis=0, concat_axis=0, tiled=True).reshape(3 * half, width)
    other = lax.ppermute(whole, "core", SWAP)
    low = jnp.where(core == 0, whole, other)
    high = jnp.where(core == 0, other, whole)

    def joined(index, base):
        cut = slice(index * half, (index + 1) * half)
        return jnp.concatenate([low[cut], high[cut]]) + base

    x_one, x_two = to_columns((-sum_one, moved_one - sum_two))
    return (x_one, joined(0, diag_one), x_two, joined(1, link_base), joined(2, two_base))


def solution(mesh):
    fine = Mesh(mesh.devices.reshape(SIZES), ALL)
    in_specs = (P(ROW, COL), P(COL, ROW), P(COL, ROW), P(), P(), P(), P(), P())
    out_specs = (P(ROW, COL), P(), P(ROW, COL), P(), P())
    return jax.shard_map(
        per_device, mesh=fine, in_specs=in_specs, out_specs=out_specs, check_vma=False
    )
```

```python
import functools

import jax
import jax.numpy as jnp
from jax import lax
from jax.experimental import pallas as pl
from jax.experimental.pallas import tpu as pltpu
from jax.sharding import Mesh, PartitionSpec as P


BLOCK = 128
ROW = ("xl", "z")
COL = ("xh", "y", "core")
PLANE = ("xh", "y")
CHIPS = ("xl", "z", "xh", "y")
ALL = ROW + COL
SIZES = (2, 4, 2, 4, 2)
SWAP = ((0, 1), (1, 0))


def product(left, right, contract=((1,), (0,))):
    return lax.dot_general(left, right, (contract, ((), ())), precision=lax.Precision.HIGH,
                           preferred_element_type=jnp.float32)


def linear(xl, z, xh, y, core):
    return (((xl * 4 + z) * 2 + xh) * 4 + y) * 2 + core


def raw_routes():
    routes = []
    for xl in range(2):
        for z in range(4):
            for xh in range(2):
                for y in range(4):
                    for core in range(2):
                        source = linear(xh, (y - z) % 4, xl, z, core)
                        routes.append((source, linear(xl, z, xh, y, core)))
    return routes


def split(value):
    high = value.astype(jnp.bfloat16)
    return high, (value - high.astype(jnp.float32)).astype(jnp.bfloat16)


def half_kernel(minus, added, kept, place_ref, a_ref, *refs):
    refs = list(refs)
    pieces = [refs.pop(0) for _ in range(8)]
    minus_ref = refs.pop(0) if minus else None
    added_ref = refs.pop(0) if added else None
    out_ref = refs.pop(0)
    factor_ref = refs.pop(0) if kept else None
    high_ref, low_ref = refs

    @pl.when(pl.program_id(0) == 0)
    def _():
        for index, piece_ref in enumerate(pieces):
            size = piece_ref.shape[0]
            span = pl.ds(pl.multiple_of(place_ref[1 + index] * size, size), size)
            value = piece_ref[...]
            if minus:
                value = value - minus_ref[span, :]
            high, low = split(value)
            if kept:
                factor_ref[span, :] = value
            high_ref[span, :] = high
            low_ref[span, :] = low

    a_high, a_low = split(a_ref[...])
    dims = (((1,), (1,)), ((), ()))
    dot = lambda l, r: lax.dot_general(l, r, dims, preferred_element_type=jnp.float32)
    total = dot(high_ref[...], a_high) + dot(low_ref[...], a_high) + dot(high_ref[...], a_low)
    out_ref[...] = total + added_ref[...] if added else total


def half_product(ancestor, pieces, places, minus=None, added=None, kept=False):
    rows, depth = ancestor.shape
    width = 8 * pieces[0].shape[0]
    tile = rows // 12
    once = dict(pipeline_mode=pl.Buffered(1))
    whole = pl.BlockSpec((width, depth), lambda i, places: (0, 0), **once)
    piece = pl.BlockSpec((width // 8, depth), lambda i, places: (0, 0), **once)
    column = pl.BlockSpec((width, tile), lambda i, places: (0, i))
    operands, in_specs = [places, ancestor, *pieces], [
        pl.BlockSpec((tile, depth), lambda i, places: (places[0] * 6 + i, 0)), *[piece] * 8]
    if minus is not None:
        operands.append(minus)
        in_specs.append(whole)
    if added is not None:
        operands.append(added)
        in_specs.append(column)
    out_shape, out_specs = [jax.ShapeDtypeStruct((width, rows // 2), jnp.float32)], [column]
    if kept:
        out_shape.append(jax.ShapeDtypeStruct((width, depth), jnp.float32))
        out_specs.append(whole)
    result = pl.pallas_call(
        functools.partial(half_kernel, minus is not None, added is not None, kept),
        grid_spec=pltpu.PrefetchScalarGridSpec(
            num_scalar_prefetch=1,
            grid=(6,),
            in_specs=in_specs,
            out_specs=out_specs,
            scratch_shapes=[pltpu.VMEM((width, depth), jnp.bfloat16)] * 2,
        ),
        out_shape=out_shape,
        cost_estimate=pl.CostEstimate(
            flops=3 * rows * depth * width, transcendentals=0,
            bytes_accessed=2 * rows * depth + 4 * width * depth + 2 * rows * width),
        compiler_params=pltpu.CompilerParams(vmem_limit_bytes=40 * 1024 * 1024),
    )(*operands)
    return result if kept else result[0]


def order_kernel(place_ref, *refs):
    pieces, (one_ref, two_ref) = refs[:8], refs[8:]
    for index, piece_ref in enumerate(pieces):
        size = piece_ref.shape[0] // 2
        span = pl.ds(pl.multiple_of(place_ref[index] * size, size), size)
        one_ref[span, :] = piece_ref[:size, :]
        two_ref[span, :] = piece_ref[size:, :]


def ordered(pieces, places):
    size, depth = pieces[0].shape
    spec = pl.BlockSpec((size, depth), lambda i, places: (0, 0), pipeline_mode=pl.Buffered(1))
    whole = pl.BlockSpec((4 * size, depth), lambda i, places: (0, 0), pipeline_mode=pl.Buffered(1))
    return pl.pallas_call(
        order_kernel,
        grid_spec=pltpu.PrefetchScalarGridSpec(
            num_scalar_prefetch=1, grid=(1,), in_specs=[spec] * 8, out_specs=[whole] * 2),
        out_shape=[jax.ShapeDtypeStruct((4 * size, depth), jnp.float32)] * 2,
        cost_estimate=pl.CostEstimate(flops=0, transcendentals=0, bytes_accessed=64 * size * depth),
        compiler_params=pltpu.CompilerParams(vmem_limit_bytes=40 * 1024 * 1024),
    )(places, *pieces)


def per_device(ancestor, lhat_one, lhat_two, link_two, diag_one, diag_two, mask_one, mask_two):
    column_index = lax.axis_index(COL)
    core = lax.axis_index("core")
    xl, z = lax.axis_index("xl"), lax.axis_index("z")
    xh, y = lax.axis_index("xh"), lax.axis_index("y")
    rows, depth = ancestor.shape
    width = link_two.shape[0]
    blocks = depth // BLOCK
    strip, half = width // 8, width // 2
    up = [(i, (i + 1) % 4) for i in range(4)]
    down = [(i, (i - 1) % 4) for i in range(4)]

    def places_of(side, ring):
        here = [side * 4 + (ring + step) % 4 for step in range(4)]
        there = [(1 - side) * 4 + (ring + step) % 4 for step in range(4)]
        return [here[0], there[0], here[3], here[1], there[3], there[1], here[2], there[2]]

    row_places = places_of(xl, z)
    own_places = jnp.stack([core] + row_places).astype(jnp.int32)
    other_places = jnp.stack([1 - core] + row_places).astype(jnp.int32)
    plane_places = jnp.stack(places_of(xh, y - z + 4)).astype(jnp.int32)

    def masked(shard, mask):
        own = lax.dynamic_slice_in_dim(mask, column_index * blocks, blocks).astype(jnp.float32)
        return shard.T * jnp.broadcast_to(own[:, None], (blocks, BLOCK)).reshape(1, depth)

    def gathered(piece, side_axis, ring_axis):
        below = lax.ppermute(piece, ring_axis, up)
        above = lax.ppermute(piece, ring_axis, down)
        side = lax.ppermute(piece, side_axis, SWAP)
        side_below = lax.ppermute(side, ring_axis, up)
        side_above = lax.ppermute(side, ring_axis, down)
        far = lax.ppermute(below, ring_axis, up)
        side_far = lax.ppermute(side_above, ring_axis, down)
        return [piece, side, below, above, side_below, side_above, far, side_far]

    def scattered(chip):
        pieces = lax.all_to_all(chip.reshape(8, strip, rows // 2), PLANE,
                                split_axis=0, concat_axis=0, tiled=True)
        return -pieces.sum(0)

    def halves(value, axis):
        size = value.shape[axis] // 2
        cut = lambda side: lax.dynamic_slice_in_dim(value, side * size, size, axis)
        return cut(core), cut(1 - core)

    def to_rows(part_t):
        keep, send = halves(part_t, 0)
        received = lax.ppermute(send, "core", SWAP)
        full = jnp.where(core == 0, jnp.concatenate([keep, received], 1),
                         jnp.concatenate([received, keep], 1))
        return full.T

    def strips(left, right):
        return product(left, right, ((1,), (1,)))

    piece_one = masked(lhat_one, mask_one)
    piece_two = masked(lhat_two, mask_two)
    pieces_one = gathered(piece_one, "xl", "z")
    raw = lax.ppermute(jnp.concatenate([piece_one, piece_two]), ALL, raw_routes())
    row_pieces = gathered(raw, "xh", "y")
    link_base = lax.optimization_barrier(-product(diag_one, link_two))
    piece_two, *pieces_one = lax.optimization_barrier((piece_two, *pieces_one))
    pieces_two = gathered(piece_two, "xl", "z")

    send_one, factor_one = half_product(ancestor, pieces_one, other_places, kept=True)
    received_one = lax.ppermute(send_one, "core", SWAP)
    chip_one = half_product(ancestor, pieces_one, own_places, added=received_one)
    x_one = scattered(chip_one)
    mixed = product(link_two, factor_one, ((0,), (0,)))
    send_two = half_product(ancestor, pieces_two, other_places, minus=mixed)
    received_two = lax.ppermute(send_two, "core", SWAP)
    chip_two = half_product(ancestor, pieces_two, own_places, minus=mixed, added=received_two)
    x_two = scattered(chip_two)

    rows_one, rows_two = ordered(row_pieces, plane_places)
    parts = jnp.stack([strips(x_one, rows_one), strips(x_one, rows_two), strips(x_two, rows_two)])
    keep, send = halves(parts, 2)
    chip = keep + lax.ppermute(send, "core", SWAP)
    chip = chip.reshape(3, 8, strip // 8, half).transpose(1, 0, 2, 3)
    piece = lax.all_to_all(chip, ROW, split_axis=0, concat_axis=0, tiled=True).sum(0)
    spread = lax.all_to_all(jnp.broadcast_to(piece[None], (64,) + piece.shape), CHIPS,
                            split_axis=0, concat_axis=0, tiled=True)
    spread = spread.reshape(8, 8, 3, strip // 8, half).transpose(2, 1, 0, 3, 4).reshape(3, width, half)
    other = lax.ppermute(spread, "core", SWAP)
    sums = jnp.where(core == 0, jnp.concatenate([spread, other], 2), jnp.concatenate([other, spread], 2))
    d_one = diag_one - sums[0].T
    link_inverse = link_base - sums[1] + product(sums[0], link_two, ((0,), (0,)))
    d_two = diag_two - sums[2].T - product(link_two, link_inverse, ((0,), (0,)))
    return (to_rows(x_one), d_one, to_rows(x_two), link_inverse, d_two)


def solution(mesh):
    fine = Mesh(mesh.devices.reshape(SIZES), ALL)
    in_specs = (P(ROW, COL), P(COL, ROW), P(COL, ROW), P(), P(), P(), P(), P())
    out_specs = (P(ROW, COL), P(), P(ROW, COL), P(), P())
    return jax.shard_map(
        per_device, mesh=fine, in_specs=in_specs, out_specs=out_specs, check_vma=False
    )
```

```python
import functools

import jax
import jax.numpy as jnp
from jax import lax
from jax.experimental import pallas as pl
from jax.experimental.pallas import tpu as pltpu
from jax.sharding import Mesh, PartitionSpec as P


BLOCK = 128
ROW = ("xl", "z")
COL = ("xh", "y", "core")
PLANE = ("xh", "y")
CHIPS = ("xl", "z", "xh", "y")
ALL = ROW + COL
SIZES = (2, 4, 2, 4, 2)
SWAP = ((0, 1), (1, 0))


def product(left, right, contract=((1,), (0,))):
    return lax.dot_general(left, right, (contract, ((), ())), precision=lax.Precision.HIGH,
                           preferred_element_type=jnp.float32)


def linear(xl, z, xh, y, core):
    return (((xl * 4 + z) * 2 + xh) * 4 + y) * 2 + core


def raw_routes():
    routes = []
    for xl in range(2):
        for z in range(4):
            for xh in range(2):
                for y in range(4):
                    for core in range(2):
                        source = linear(xh, (y - z) % 4, xl, z, core)
                        routes.append((source, linear(xl, z, xh, y, core)))
    return routes


def split(value):
    high = value.astype(jnp.bfloat16)
    return high, (value - high.astype(jnp.float32)).astype(jnp.bfloat16)


def half_kernel(minus, added, kept, place_ref, a_ref, *refs):
    refs = list(refs)
    pieces = [refs.pop(0) for _ in range(8)]
    minus_ref = refs.pop(0) if minus else None
    added_ref = refs.pop(0) if added else None
    out_ref = refs.pop(0)
    factor_ref = refs.pop(0) if kept else None
    (both_ref,) = refs
    width = both_ref.shape[0] // 2

    @pl.when(pl.program_id(0) == 0)
    def _():
        for index, piece_ref in enumerate(pieces):
            size = piece_ref.shape[0]
            start = pl.multiple_of(place_ref[1 + index] * size, size)
            span = pl.ds(start, size)
            value = piece_ref[...]
            if minus:
                value = value - minus_ref[span, :]
            high, low = split(value)
            if kept:
                factor_ref[span, :] = value
            both_ref[span, :] = high
            both_ref[pl.ds(pl.multiple_of(start + width, size), size), :] = low

    a_high, a_low = split(a_ref[...])
    dims = (((1,), (1,)), ((), ()))
    dot = lambda l, r: lax.dot_general(l, r, dims, preferred_element_type=jnp.float32)
    stacked = dot(both_ref[...], a_high)
    total = stacked[:width] + stacked[width:] + dot(both_ref[:width, :], a_low)
    out_ref[...] = total + added_ref[...] if added else total


def half_product(ancestor, pieces, places, minus=None, added=None, kept=False):
    rows, depth = ancestor.shape
    width = 8 * pieces[0].shape[0]
    tile = rows // 12
    once = dict(pipeline_mode=pl.Buffered(1))
    whole = pl.BlockSpec((width, depth), lambda i, places: (0, 0), **once)
    piece = pl.BlockSpec((width // 8, depth), lambda i, places: (0, 0), **once)
    column = pl.BlockSpec((width, tile), lambda i, places: (0, i))
    operands, in_specs = [places, ancestor, *pieces], [
        pl.BlockSpec((tile, depth), lambda i, places: (places[0] * 6 + i, 0)), *[piece] * 8]
    if minus is not None:
        operands.append(minus)
        in_specs.append(whole)
    if added is not None:
        operands.append(added)
        in_specs.append(column)
    out_shape, out_specs = [jax.ShapeDtypeStruct((width, rows // 2), jnp.float32)], [column]
    if kept:
        out_shape.append(jax.ShapeDtypeStruct((width, depth), jnp.float32))
        out_specs.append(whole)
    result = pl.pallas_call(
        functools.partial(half_kernel, minus is not None, added is not None, kept),
        grid_spec=pltpu.PrefetchScalarGridSpec(
            num_scalar_prefetch=1,
            grid=(6,),
            in_specs=in_specs,
            out_specs=out_specs,
            scratch_shapes=[pltpu.VMEM((2 * width, depth), jnp.bfloat16)],
        ),
        out_shape=out_shape,
        cost_estimate=pl.CostEstimate(
            flops=3 * rows * depth * width, transcendentals=0,
            bytes_accessed=2 * rows * depth + 4 * width * depth + 2 * rows * width),
        compiler_params=pltpu.CompilerParams(vmem_limit_bytes=60 * 1024 * 1024),
    )(*operands)
    return result if kept else result[0]


def order_kernel(place_ref, *refs):
    pieces, (one_ref, two_ref) = refs[:8], refs[8:]
    for index, piece_ref in enumerate(pieces):
        size = piece_ref.shape[0] // 2
        span = pl.ds(pl.multiple_of(place_ref[index] * size, size), size)
        one_ref[span, :] = piece_ref[:size, :]
        two_ref[span, :] = piece_ref[size:, :]


def ordered(pieces, places):
    size, depth = pieces[0].shape
    spec = pl.BlockSpec((size, depth), lambda i, places: (0, 0), pipeline_mode=pl.Buffered(1))
    whole = pl.BlockSpec((4 * size, depth), lambda i, places: (0, 0), pipeline_mode=pl.Buffered(1))
    return pl.pallas_call(
        order_kernel,
        grid_spec=pltpu.PrefetchScalarGridSpec(
            num_scalar_prefetch=1, grid=(1,), in_specs=[spec] * 8, out_specs=[whole] * 2),
        out_shape=[jax.ShapeDtypeStruct((4 * size, depth), jnp.float32)] * 2,
        cost_estimate=pl.CostEstimate(flops=0, transcendentals=0, bytes_accessed=64 * size * depth),
        compiler_params=pltpu.CompilerParams(vmem_limit_bytes=40 * 1024 * 1024),
    )(places, *pieces)


def per_device(ancestor, lhat_one, lhat_two, link_two, diag_one, diag_two, mask_one, mask_two):
    column_index = lax.axis_index(COL)
    core = lax.axis_index("core")
    xl, z = lax.axis_index("xl"), lax.axis_index("z")
    xh, y = lax.axis_index("xh"), lax.axis_index("y")
    rows, depth = ancestor.shape
    width = link_two.shape[0]
    blocks = depth // BLOCK
    strip, half = width // 8, width // 2
    up = [(i, (i + 1) % 4) for i in range(4)]
    down = [(i, (i - 1) % 4) for i in range(4)]

    def places_of(side, ring):
        here = [side * 4 + (ring + step) % 4 for step in range(4)]
        there = [(1 - side) * 4 + (ring + step) % 4 for step in range(4)]
        return [here[0], there[0], here[3], here[1], there[3], there[1], here[2], there[2]]

    row_places = places_of(xl, z)
    own_places = jnp.stack([core] + row_places).astype(jnp.int32)
    other_places = jnp.stack([1 - core] + row_places).astype(jnp.int32)
    plane_places = jnp.stack(places_of(xh, y - z + 4)).astype(jnp.int32)

    def masked(shard, mask):
        own = lax.dynamic_slice_in_dim(mask, column_index * blocks, blocks).astype(jnp.float32)
        return shard.T * jnp.broadcast_to(own[:, None], (blocks, BLOCK)).reshape(1, depth)

    def gathered(piece, side_axis, ring_axis, side=None):
        below = lax.ppermute(piece, ring_axis, up)
        above = lax.ppermute(piece, ring_axis, down)
        if side is None:
            side = lax.ppermute(piece, side_axis, SWAP)
        side_below = lax.ppermute(side, ring_axis, up)
        side_above = lax.ppermute(side, ring_axis, down)
        far = lax.ppermute(below, ring_axis, up)
        side_far = lax.ppermute(side_above, ring_axis, down)
        return [piece, side, below, above, side_below, side_above, far, side_far]

    def scattered(chip):
        pieces = lax.all_to_all(chip.reshape(8, strip, rows // 2), PLANE,
                                split_axis=0, concat_axis=0, tiled=True)
        return -pieces.sum(0)

    def halves(value, axis):
        size = value.shape[axis] // 2
        cut = lambda side: lax.dynamic_slice_in_dim(value, side * size, size, axis)
        return cut(core), cut(1 - core)

    def to_rows(part_t):
        keep, send = halves(part_t, 0)
        received = lax.ppermute(send, "core", SWAP)
        full = jnp.where(core == 0, jnp.concatenate([keep, received], 1),
                         jnp.concatenate([received, keep], 1))
        return full.T

    def strips(left, right):
        return product(left, right, ((1,), (1,)))

    piece_one = masked(lhat_one, mask_one)
    piece_two = masked(lhat_two, mask_two)
    pieces_one = gathered(piece_one, "xl", "z")
    raw = lax.ppermute(jnp.concatenate([piece_one, piece_two]), ALL, raw_routes())
    row_pieces = gathered(raw, "xh", "y")
    link_base, one_base, two_base = lax.optimization_barrier(
        (-product(diag_one, link_two), diag_one.T, diag_two.T))
    side_two = lax.ppermute(piece_two, "xl", SWAP)
    piece_two, side_two, *pieces_one = lax.optimization_barrier((piece_two, side_two, *pieces_one))
    pieces_two = gathered(piece_two, "xl", "z", side_two)

    send_one, factor_one = half_product(ancestor, pieces_one, other_places, kept=True)
    received_one = lax.ppermute(send_one, "core", SWAP)
    chip_one = half_product(ancestor, pieces_one, own_places, added=received_one)
    x_one = scattered(chip_one)
    mixed = product(link_two, factor_one, ((0,), (0,)))
    send_two = half_product(ancestor, pieces_two, other_places, minus=mixed)
    received_two = lax.ppermute(send_two, "core", SWAP)
    chip_two = half_product(ancestor, pieces_two, own_places, minus=mixed, added=received_two)
    x_two = scattered(chip_two)

    rows_one, rows_two = ordered(row_pieces, plane_places)
    parts = jnp.stack([strips(x_one, rows_one), strips(x_one, rows_two), strips(x_two, rows_two)])
    keep, send = halves(parts, 2)
    chip = keep + lax.ppermute(send, "core", SWAP)
    chip = chip.reshape(3, 8, strip // 8, half).transpose(1, 0, 2, 3)
    piece = lax.all_to_all(chip, ROW, split_axis=0, concat_axis=0, tiled=True).sum(0)
    spread = lax.all_to_all(jnp.broadcast_to(piece[None], (64,) + piece.shape), CHIPS,
                            split_axis=0, concat_axis=0, tiled=True)
    spread = spread.reshape(8, 8, 3, strip // 8, half).transpose(2, 1, 0, 3, 4).reshape(3, width, half)
    other = lax.ppermute(spread, "core", SWAP)
    sums = jnp.where(core == 0, jnp.concatenate([spread, other], 2), jnp.concatenate([other, spread], 2))
    d_one = (one_base - sums[0]).T
    link_inverse = link_base - sums[1] + product(sums[0], link_two, ((0,), (0,)))
    d_two = (two_base - sums[2] - product(link_inverse, link_two, ((0,), (0,)))).T
    return (to_rows(x_one), d_one, to_rows(x_two), link_inverse, d_two)


def solution(mesh):
    fine = Mesh(mesh.devices.reshape(SIZES), ALL)
    in_specs = (P(ROW, COL), P(COL, ROW), P(COL, ROW), P(), P(), P(), P(), P())
    out_specs = (P(ROW, COL), P(), P(ROW, COL), P(), P())
    return jax.shard_map(
        per_device, mesh=fine, in_specs=in_specs, out_specs=out_specs, check_vma=False
    )
```

```python
import functools

import jax
import jax.numpy as jnp
from jax import lax
from jax.experimental import pallas as pl
from jax.experimental.pallas import tpu as pltpu
from jax.sharding import Mesh, PartitionSpec as P


BLOCK = 128
LIMIT = 60 * 1024 * 1024
ROW = ("xl", "z")
COL = ("xh", "y", "core")
PLANE = ("xh", "y")
CHIPS = ("xl", "z", "xh", "y")
ALL = ROW + COL
SIZES = (2, 4, 2, 4, 2)
SWAP = ((0, 1), (1, 0))


def product(left, right, contract=((1,), (0,))):
    return lax.dot_general(left, right, (contract, ((), ())), precision=lax.Precision.HIGH,
                           preferred_element_type=jnp.float32)


def linear(xl, z, xh, y, core):
    return (((xl * 4 + z) * 2 + xh) * 4 + y) * 2 + core


def raw_routes():
    routes = []
    for xl in range(2):
        for z in range(4):
            for xh in range(2):
                for y in range(4):
                    for core in range(2):
                        source = linear(xh, (y - z) % 4, xl, z, core)
                        routes.append((source, linear(xl, z, xh, y, core)))
    return routes


def split(value):
    high = value.astype(jnp.bfloat16)
    return high, (value - high.astype(jnp.float32)).astype(jnp.bfloat16)


def half_kernel(minus, added, kept, place_ref, a_ref, *refs):
    refs = list(refs)
    pieces = [refs.pop(0) for _ in range(8)]
    minus_ref = refs.pop(0) if minus else None
    added_ref = refs.pop(0) if added else None
    out_ref = refs.pop(0)
    factor_ref = refs.pop(0) if kept else None
    high_ref, low_ref, stage_ref, sems = refs[:4]
    taken_ref, taken_sems = refs[4:] if minus else (None, None)
    size = pieces[0].shape[0]

    @pl.when(pl.program_id(0) == 0)
    def _():
        spans = [pl.ds(pl.multiple_of(place_ref[1 + index] * size, size), size) for index in range(8)]
        copies = []
        for index in range(8):
            group = [pltpu.make_async_copy(pieces[index], stage_ref.at[index], sems.at[index])]
            if minus:
                group.append(pltpu.make_async_copy(
                    minus_ref.at[spans[index], :], taken_ref.at[index], taken_sems.at[index]))
            for copy in group:
                copy.start()
            copies.append(group)
        for index, span in enumerate(spans):
            for copy in copies[index]:
                copy.wait()
            value = stage_ref[index]
            if minus:
                value = value - taken_ref[index]
            high, low = split(value)
            if kept:
                factor_ref[span, :] = value
            high_ref[span, :] = high
            low_ref[span, :] = low

    a_high, a_low = split(a_ref[...])
    dims = (((1,), (1,)), ((), ()))
    dot = lambda l, r: lax.dot_general(l, r, dims, preferred_element_type=jnp.float32)
    total = dot(high_ref[...], a_high) + dot(low_ref[...], a_high) + dot(high_ref[...], a_low)
    out_ref[...] = total + added_ref[...] if added else total


def half_product(ancestor, pieces, places, minus=None, added=None, kept=False):
    rows, depth = ancestor.shape
    width = 8 * pieces[0].shape[0]
    tile = rows // 12
    once = dict(pipeline_mode=pl.Buffered(1))
    whole = pl.BlockSpec((width, depth), lambda i, places: (0, 0), **once)
    anywhere = pl.BlockSpec(memory_space=pl.ANY)
    stage = [pltpu.VMEM((8, width // 8, depth), jnp.float32), pltpu.SemaphoreType.DMA((8,))]
    column = pl.BlockSpec((width, tile), lambda i, places: (0, i))
    operands, in_specs = [places, ancestor, *pieces], [
        pl.BlockSpec((tile, depth), lambda i, places: (places[0] * 6 + i, 0)), *[anywhere] * 8]
    if minus is not None:
        operands.append(minus)
        in_specs.append(anywhere)
    if added is not None:
        operands.append(added)
        in_specs.append(column)
    out_shape, out_specs = [jax.ShapeDtypeStruct((width, rows // 2), jnp.float32)], [column]
    if kept:
        out_shape.append(jax.ShapeDtypeStruct((width, depth), jnp.float32))
        out_specs.append(whole)
    result = pl.pallas_call(
        functools.partial(half_kernel, minus is not None, added is not None, kept),
        grid_spec=pltpu.PrefetchScalarGridSpec(
            num_scalar_prefetch=1,
            grid=(6,),
            in_specs=in_specs,
            out_specs=out_specs,
            scratch_shapes=[pltpu.VMEM((width, depth), jnp.bfloat16)] * 2 + stage * (1 if minus is None else 2),
        ),
        out_shape=out_shape,
        cost_estimate=pl.CostEstimate(
            flops=3 * rows * depth * width, transcendentals=0,
            bytes_accessed=2 * rows * depth + 4 * width * depth + 2 * rows * width),
        compiler_params=pltpu.CompilerParams(vmem_limit_bytes=LIMIT),
    )(*operands)
    return result if kept else result[0]


def order_kernel(place_ref, *refs):
    pieces, (one_ref, two_ref) = refs[:8], refs[8:]
    for index, piece_ref in enumerate(pieces):
        size = piece_ref.shape[0] // 2
        span = pl.ds(pl.multiple_of(place_ref[index] * size, size), size)
        one_ref[span, :] = piece_ref[:size, :]
        two_ref[span, :] = piece_ref[size:, :]


def ordered(pieces, places):
    size, depth = pieces[0].shape
    spec = pl.BlockSpec((size, depth), lambda i, places: (0, 0), pipeline_mode=pl.Buffered(1))
    whole = pl.BlockSpec((4 * size, depth), lambda i, places: (0, 0), pipeline_mode=pl.Buffered(1))
    return pl.pallas_call(
        order_kernel,
        grid_spec=pltpu.PrefetchScalarGridSpec(
            num_scalar_prefetch=1, grid=(1,), in_specs=[spec] * 8, out_specs=[whole] * 2),
        out_shape=[jax.ShapeDtypeStruct((4 * size, depth), jnp.float32)] * 2,
        cost_estimate=pl.CostEstimate(flops=0, transcendentals=0, bytes_accessed=64 * size * depth),
        compiler_params=pltpu.CompilerParams(vmem_limit_bytes=40 * 1024 * 1024),
    )(places, *pieces)


def per_device(ancestor, lhat_one, lhat_two, link_two, diag_one, diag_two, mask_one, mask_two):
    column_index = lax.axis_index(COL)
    core = lax.axis_index("core")
    xl, z = lax.axis_index("xl"), lax.axis_index("z")
    xh, y = lax.axis_index("xh"), lax.axis_index("y")
    rows, depth = ancestor.shape
    width = link_two.shape[0]
    blocks = depth // BLOCK
    strip, half = width // 8, width // 2
    up = [(i, (i + 1) % 4) for i in range(4)]
    down = [(i, (i - 1) % 4) for i in range(4)]

    def places_of(side, ring):
        here = [side * 4 + (ring + step) % 4 for step in range(4)]
        there = [(1 - side) * 4 + (ring + step) % 4 for step in range(4)]
        return [here[0], there[0], here[3], here[1], there[3], there[1], here[2], there[2]]

    row_places = places_of(xl, z)
    own_places = jnp.stack([core] + row_places).astype(jnp.int32)
    other_places = jnp.stack([1 - core] + row_places).astype(jnp.int32)
    plane_places = jnp.stack(places_of(xh, y - z + 4)).astype(jnp.int32)

    def masked(shard, mask):
        own = lax.dynamic_slice_in_dim(mask, column_index * blocks, blocks).astype(jnp.float32)
        return shard.T * jnp.broadcast_to(own[:, None], (blocks, BLOCK)).reshape(1, depth)

    def gathered(piece, side_axis, ring_axis, side=None):
        below = lax.ppermute(piece, ring_axis, up)
        above = lax.ppermute(piece, ring_axis, down)
        if side is None:
            side = lax.ppermute(piece, side_axis, SWAP)
        side_below = lax.ppermute(side, ring_axis, up)
        side_above = lax.ppermute(side, ring_axis, down)
        far = lax.ppermute(below, ring_axis, up)
        side_far = lax.ppermute(side_above, ring_axis, down)
        return [piece, side, below, above, side_below, side_above, far, side_far]

    def scattered(chip):
        pieces = lax.all_to_all(chip.reshape(8, strip, rows // 2), PLANE,
                                split_axis=0, concat_axis=0, tiled=True)
        return -pieces.sum(0)

    def halves(value, axis):
        size = value.shape[axis] // 2
        cut = lambda side: lax.dynamic_slice_in_dim(value, side * size, size, axis)
        return cut(core), cut(1 - core)

    def to_rows(part_t):
        keep, send = halves(part_t, 0)
        received = lax.ppermute(send, "core", SWAP)
        full = jnp.where(core == 0, jnp.concatenate([keep, received], 1),
                         jnp.concatenate([received, keep], 1))
        return full.T

    def strips(left, right):
        return product(left, right, ((1,), (1,)))

    piece_one = masked(lhat_one, mask_one)
    piece_two = masked(lhat_two, mask_two)
    pieces_one = gathered(piece_one, "xl", "z")
    raw = lax.ppermute(jnp.concatenate([piece_one, piece_two]), ALL, raw_routes())
    row_pieces = gathered(raw, "xh", "y")
    link_base = lax.optimization_barrier(-product(diag_one, link_two))
    side_two = lax.ppermute(piece_two, "xl", SWAP)
    piece_two, side_two, *pieces_one = lax.optimization_barrier((piece_two, side_two, *pieces_one))
    pieces_two = gathered(piece_two, "xl", "z", side_two)

    send_one, factor_one = half_product(ancestor, pieces_one, other_places, kept=True)
    received_one = lax.ppermute(send_one, "core", SWAP)
    chip_one = half_product(ancestor, pieces_one, own_places, added=received_one)
    x_one = scattered(chip_one)
    mixed = product(link_two, factor_one, ((0,), (0,)))
    send_two = half_product(ancestor, pieces_two, other_places, minus=mixed)
    received_two = lax.ppermute(send_two, "core", SWAP)
    chip_two = half_product(ancestor, pieces_two, own_places, minus=mixed, added=received_two)
    x_two = scattered(chip_two)

    rows_one, rows_two = ordered(row_pieces, plane_places)
    parts = jnp.stack([strips(x_one, rows_one), strips(x_one, rows_two), strips(x_two, rows_two)])
    keep, send = halves(parts, 2)
    chip = keep + lax.ppermute(send, "core", SWAP)
    chip = chip.reshape(3, 8, strip // 8, half).transpose(1, 0, 2, 3)
    piece = lax.all_to_all(chip, ROW, split_axis=0, concat_axis=0, tiled=True).sum(0)
    spread = lax.all_to_all(jnp.broadcast_to(piece[None], (64,) + piece.shape), CHIPS,
                            split_axis=0, concat_axis=0, tiled=True)
    spread = spread.reshape(8, 8, 3, strip // 8, half).transpose(2, 1, 0, 3, 4).reshape(3, width, half)
    other = lax.ppermute(spread, "core", SWAP)
    sums = jnp.where(core == 0, jnp.concatenate([spread, other], 2), jnp.concatenate([other, spread], 2))
    turned_one, turned_two = lax.optimization_barrier((sums[0].T, sums[2].T))
    d_one = diag_one - turned_one
    link_inverse = link_base - sums[1] + product(sums[0], link_two, ((0,), (0,)))
    d_two = diag_two - turned_two - product(link_two, link_inverse, ((0,), (0,)))
    return (to_rows(x_one), d_one, to_rows(x_two), link_inverse, d_two)


def solution(mesh):
    fine = Mesh(mesh.devices.reshape(SIZES), ALL)
    in_specs = (P(ROW, COL), P(COL, ROW), P(COL, ROW), P(), P(), P(), P(), P())
    out_specs = (P(ROW, COL), P(), P(ROW, COL), P(), P())
    return jax.shard_map(
        per_device, mesh=fine, in_specs=in_specs, out_specs=out_specs, check_vma=False
    )
```

```python
import functools

import jax
import jax.numpy as jnp
from jax import lax
from jax.experimental import pallas as pl
from jax.experimental.pallas import tpu as pltpu
from jax.sharding import Mesh, PartitionSpec as P


BLOCK = 128
LIMIT = 32 * 1024 * 1024
ROW = ("xl", "z")
COL = ("xh", "y", "core")
PLANE = ("xh", "y")
CHIPS = ("xl", "z", "xh", "y")
ALL = ROW + COL
SIZES = (2, 4, 2, 4, 2)
SWAP = ((0, 1), (1, 0))


def product(left, right, contract=((1,), (0,))):
    return lax.dot_general(left, right, (contract, ((), ())), precision=lax.Precision.HIGH,
                           preferred_element_type=jnp.float32)


def linear(xl, z, xh, y, core):
    return (((xl * 4 + z) * 2 + xh) * 4 + y) * 2 + core


def raw_routes():
    routes = []
    for xl in range(2):
        for z in range(4):
            for xh in range(2):
                for y in range(4):
                    for core in range(2):
                        source = linear(xh, (y - z) % 4, xl, z, core)
                        routes.append((source, linear(xl, z, xh, y, core)))
    return routes


def split(value):
    high = value.astype(jnp.bfloat16)
    return high, (value - high.astype(jnp.float32)).astype(jnp.bfloat16)


def multiply(a_ref, high_ref, low_ref):
    a_high, a_low = split(a_ref[...])
    dims = (((1,), (1,)), ((), ()))
    dot = lambda l, r: lax.dot_general(l, r, dims, preferred_element_type=jnp.float32)
    return dot(high_ref[...], a_high) + dot(low_ref[...], a_high) + dot(high_ref[...], a_low)


def first_kernel(minus, kept, place_ref, a_ref, *refs):
    refs = list(refs)
    pieces = [refs.pop(0) for _ in range(8)]
    minus_ref = refs.pop(0) if minus else None
    out_ref, high_ref, low_ref = refs[:3]
    factor_ref = refs[3] if kept else None

    @pl.when(pl.program_id(0) == 0)
    def _():
        for index, piece_ref in enumerate(pieces):
            size = piece_ref.shape[0]
            span = pl.ds(pl.multiple_of(place_ref[1 + index] * size, size), size)
            value = piece_ref[...]
            if minus:
                value = value - minus_ref[span, :]
            high, low = split(value)
            if kept:
                factor_ref[span, :] = value
            high_ref[span, :] = high
            low_ref[span, :] = low

    out_ref[...] = multiply(a_ref, high_ref, low_ref)


def second_kernel(place_ref, a_ref, high_ref, low_ref, added_ref, out_ref):
    del place_ref
    out_ref[...] = multiply(a_ref, high_ref, low_ref) + added_ref[...]


def half_product(ancestor, places, pieces=None, minus=None, kept=False, parts=None, added=None):
    rows, depth = ancestor.shape
    width = 8 * pieces[0].shape[0] if pieces else parts[0].shape[0]
    tile = rows // 12
    once = dict(pipeline_mode=pl.Buffered(1))
    whole = pl.BlockSpec((width, depth), lambda i, places: (0, 0), **once)
    piece = pl.BlockSpec((width // 8, depth), lambda i, places: (0, 0), **once)
    column = pl.BlockSpec((width, tile), lambda i, places: (0, i))
    in_specs = [pl.BlockSpec((tile, depth), lambda i, places: (places[0] * 6 + i, 0))]
    out_shape, out_specs = [jax.ShapeDtypeStruct((width, rows // 2), jnp.float32)], [column]
    if pieces:
        kernel = functools.partial(first_kernel, minus is not None, kept)
        operands = [*pieces] + ([] if minus is None else [minus])
        in_specs += [piece] * 8 + ([] if minus is None else [whole])
        for kind in [jnp.bfloat16, jnp.bfloat16] + [jnp.float32] * kept:
            out_shape.append(jax.ShapeDtypeStruct((width, depth), kind))
            out_specs.append(whole)
    else:
        kernel = second_kernel
        operands = [*parts, added]
        in_specs += [whole, whole, column]
    return pl.pallas_call(
        kernel,
        grid_spec=pltpu.PrefetchScalarGridSpec(
            num_scalar_prefetch=1, grid=(6,), in_specs=in_specs, out_specs=out_specs),
        out_shape=out_shape,
        cost_estimate=pl.CostEstimate(
            flops=3 * rows * depth * width, transcendentals=0,
            bytes_accessed=2 * rows * depth + 4 * width * depth + 2 * rows * width),
        compiler_params=pltpu.CompilerParams(vmem_limit_bytes=LIMIT),
    )(places, ancestor, *operands)


def order_kernel(place_ref, *refs):
    pieces, (one_ref, two_ref) = refs[:8], refs[8:]
    for index, piece_ref in enumerate(pieces):
        size = piece_ref.shape[0] // 2
        span = pl.ds(pl.multiple_of(place_ref[index] * size, size), size)
        one_ref[span, :] = piece_ref[:size, :]
        two_ref[span, :] = piece_ref[size:, :]


def ordered(pieces, places):
    size, depth = pieces[0].shape
    spec = pl.BlockSpec((size, depth), lambda i, places: (0, 0), pipeline_mode=pl.Buffered(1))
    whole = pl.BlockSpec((4 * size, depth), lambda i, places: (0, 0), pipeline_mode=pl.Buffered(1))
    return pl.pallas_call(
        order_kernel,
        grid_spec=pltpu.PrefetchScalarGridSpec(
            num_scalar_prefetch=1, grid=(1,), in_specs=[spec] * 8, out_specs=[whole] * 2),
        out_shape=[jax.ShapeDtypeStruct((4 * size, depth), jnp.float32)] * 2,
        cost_estimate=pl.CostEstimate(flops=0, transcendentals=0, bytes_accessed=64 * size * depth),
        compiler_params=pltpu.CompilerParams(vmem_limit_bytes=40 * 1024 * 1024),
    )(places, *pieces)


def per_device(ancestor, lhat_one, lhat_two, link_two, diag_one, diag_two, mask_one, mask_two):
    column_index = lax.axis_index(COL)
    core = lax.axis_index("core")
    xl, z = lax.axis_index("xl"), lax.axis_index("z")
    xh, y = lax.axis_index("xh"), lax.axis_index("y")
    rows, depth = ancestor.shape
    width = link_two.shape[0]
    blocks = depth // BLOCK
    strip, half = width // 8, width // 2
    up = [(i, (i + 1) % 4) for i in range(4)]
    down = [(i, (i - 1) % 4) for i in range(4)]

    def places_of(side, ring):
        here = [side * 4 + (ring + step) % 4 for step in range(4)]
        there = [(1 - side) * 4 + (ring + step) % 4 for step in range(4)]
        return [here[0], there[0], here[3], here[1], there[3], there[1], here[2], there[2]]

    row_places = places_of(xl, z)
    own_places = jnp.stack([core] + row_places).astype(jnp.int32)
    other_places = jnp.stack([1 - core] + row_places).astype(jnp.int32)
    plane_places = jnp.stack(places_of(xh, y - z + 4)).astype(jnp.int32)

    def masked(shard, mask):
        own = lax.dynamic_slice_in_dim(mask, column_index * blocks, blocks).astype(jnp.float32)
        return shard.T * jnp.broadcast_to(own[:, None], (blocks, BLOCK)).reshape(1, depth)

    def gathered(piece, side_axis, ring_axis):
        below = lax.ppermute(piece, ring_axis, up)
        above = lax.ppermute(piece, ring_axis, down)
        side = lax.ppermute(piece, side_axis, SWAP)
        side_below = lax.ppermute(side, ring_axis, up)
        side_above = lax.ppermute(side, ring_axis, down)
        far = lax.ppermute(below, ring_axis, up)
        side_far = lax.ppermute(side_above, ring_axis, down)
        return [piece, side, below, above, side_below, side_above, far, side_far]

    def scattered(chip):
        pieces = lax.all_to_all(chip.reshape(8, strip, rows // 2), PLANE,
                                split_axis=0, concat_axis=0, tiled=True)
        return -pieces.sum(0)

    def halves(value, axis):
        size = value.shape[axis] // 2
        cut = lambda side: lax.dynamic_slice_in_dim(value, side * size, size, axis)
        return cut(core), cut(1 - core)

    def to_rows(part_t):
        keep, send = halves(part_t, 0)
        received = lax.ppermute(send, "core", SWAP)
        full = jnp.where(core == 0, jnp.concatenate([keep, received], 1),
                         jnp.concatenate([received, keep], 1))
        return full.T

    def strips(left, right):
        return product(left, right, ((1,), (1,)))

    piece_one = masked(lhat_one, mask_one)
    piece_two = masked(lhat_two, mask_two)
    pieces_one = gathered(piece_one, "xl", "z")
    raw = lax.ppermute(jnp.concatenate([piece_one, piece_two]), ALL, raw_routes())
    row_pieces = gathered(raw, "xh", "y")
    link_base = lax.optimization_barrier(-product(diag_one, link_two))
    piece_two, *pieces_one = lax.optimization_barrier((piece_two, *pieces_one))
    pieces_two = gathered(piece_two, "xl", "z")

    send_one, *parts_one, factor_one = half_product(ancestor, other_places, pieces_one, kept=True)
    received_one = lax.ppermute(send_one, "core", SWAP)
    (chip_one,) = half_product(ancestor, own_places, parts=parts_one, added=received_one)
    x_one = scattered(chip_one)
    mixed = product(link_two, factor_one, ((0,), (0,)))
    send_two, *parts_two = half_product(ancestor, other_places, pieces_two, minus=mixed)
    received_two = lax.ppermute(send_two, "core", SWAP)
    (chip_two,) = half_product(ancestor, own_places, parts=parts_two, added=received_two)
    x_two = scattered(chip_two)

    rows_one, rows_two = ordered(row_pieces, plane_places)
    parts = jnp.stack([strips(x_one, rows_one), strips(x_one, rows_two), strips(x_two, rows_two)])
    keep, send = halves(parts, 2)
    chip = keep + lax.ppermute(send, "core", SWAP)
    chip = chip.reshape(3, 8, strip // 8, half).transpose(1, 0, 2, 3)
    piece = lax.all_to_all(chip, ROW, split_axis=0, concat_axis=0, tiled=True).sum(0)
    spread = lax.all_to_all(jnp.broadcast_to(piece[None], (64,) + piece.shape), CHIPS,
                            split_axis=0, concat_axis=0, tiled=True)
    spread = spread.reshape(8, 8, 3, strip // 8, half).transpose(2, 1, 0, 3, 4).reshape(3, width, half)
    other = lax.ppermute(spread, "core", SWAP)
    sums = jnp.where(core == 0, jnp.concatenate([spread, other], 2), jnp.concatenate([other, spread], 2))
    d_one = diag_one - sums[0].T
    link_inverse = link_base - sums[1] + product(sums[0], link_two, ((0,), (0,)))
    d_two = diag_two - sums[2].T - product(link_two, link_inverse, ((0,), (0,)))
    return (to_rows(x_one), d_one, to_rows(x_two), link_inverse, d_two)


def solution(mesh):
    fine = Mesh(mesh.devices.reshape(SIZES), ALL)
    in_specs = (P(ROW, COL), P(COL, ROW), P(COL, ROW), P(), P(), P(), P(), P())
    out_specs = (P(ROW, COL), P(), P(ROW, COL), P(), P())
    return jax.shard_map(
        per_device, mesh=fine, in_specs=in_specs, out_specs=out_specs, check_vma=False
    )
```

```python
import functools

import jax
import jax.numpy as jnp
from jax import lax
from jax.experimental import pallas as pl
from jax.experimental.pallas import tpu as pltpu
from jax.sharding import Mesh, PartitionSpec as P


BLOCK = 128
LIMIT = 32 * 1024 * 1024
ROW = ("xl", "z")
COL = ("xh", "y", "core")
PLANE = ("xh", "y")
CHIPS = ("xl", "z", "xh", "y")
ALL = ROW + COL
SIZES = (2, 4, 2, 4, 2)
SWAP = ((0, 1), (1, 0))


def product(left, right, contract=((1,), (0,))):
    return lax.dot_general(left, right, (contract, ((), ())), precision=lax.Precision.HIGH,
                           preferred_element_type=jnp.float32)


def linear(xl, z, xh, y, core):
    return (((xl * 4 + z) * 2 + xh) * 4 + y) * 2 + core


def raw_routes():
    routes = []
    for xl in range(2):
        for z in range(4):
            for xh in range(2):
                for y in range(4):
                    for core in range(2):
                        source = linear(xh, (y - z) % 4, xl, z, core)
                        routes.append((source, linear(xl, z, xh, y, core)))
    return routes


def split(value):
    high = value.astype(jnp.bfloat16)
    return high, (value - high.astype(jnp.float32)).astype(jnp.bfloat16)


def multiply(a_ref, high_ref, low_ref):
    a_high, a_low = split(a_ref[...])
    dims = (((1,), (1,)), ((), ()))
    dot = lambda l, r: lax.dot_general(l, r, dims, preferred_element_type=jnp.float32)
    return dot(high_ref[...], a_high) + dot(low_ref[...], a_high) + dot(high_ref[...], a_low)


def first_kernel(minus, kept, place_ref, a_ref, *refs):
    refs = list(refs)
    pieces = [refs.pop(0) for _ in range(8)]
    minus_ref = refs.pop(0) if minus else None
    out_ref, high_ref, low_ref = refs[:3]
    factor_ref = refs[3] if kept else None

    @pl.when(pl.program_id(0) == 0)
    def _():
        for index, piece_ref in enumerate(pieces):
            size = piece_ref.shape[0]
            span = pl.ds(pl.multiple_of(place_ref[1 + index] * size, size), size)
            value = piece_ref[...]
            if minus:
                value = value - minus_ref[span, :]
            high, low = split(value)
            if kept:
                factor_ref[span, :] = value
            high_ref[span, :] = high
            low_ref[span, :] = low

    out_ref[...] = multiply(a_ref, high_ref, low_ref)


def second_kernel(place_ref, a_ref, high_ref, low_ref, added_ref, out_ref):
    del place_ref
    out_ref[...] = multiply(a_ref, high_ref, low_ref) + added_ref[...]


def half_product(ancestor, places, pieces=None, minus=None, kept=False, parts=None, added=None):
    rows, depth = ancestor.shape
    width = 8 * pieces[0].shape[0] if pieces else parts[0].shape[0]
    tile = rows // 12
    once = dict(pipeline_mode=pl.Buffered(1))
    whole = pl.BlockSpec((width, depth), lambda i, places: (0, 0), **once)
    piece = pl.BlockSpec((width // 8, depth), lambda i, places: (0, 0), **once)
    column = pl.BlockSpec((width, tile), lambda i, places: (0, i))
    in_specs = [pl.BlockSpec((tile, depth), lambda i, places: (places[0] * 6 + i, 0))]
    out_shape, out_specs = [jax.ShapeDtypeStruct((width, rows // 2), jnp.float32)], [column]
    if pieces:
        kernel = functools.partial(first_kernel, minus is not None, kept)
        operands = [*pieces] + ([] if minus is None else [minus])
        in_specs += [piece] * 8 + ([] if minus is None else [whole])
        for kind in [jnp.bfloat16, jnp.bfloat16] + [jnp.float32] * kept:
            out_shape.append(jax.ShapeDtypeStruct((width, depth), kind))
            out_specs.append(whole)
    else:
        kernel = second_kernel
        operands = [*parts, added]
        in_specs += [whole, whole, column]
    return pl.pallas_call(
        kernel,
        grid_spec=pltpu.PrefetchScalarGridSpec(
            num_scalar_prefetch=1, grid=(6,), in_specs=in_specs, out_specs=out_specs),
        out_shape=out_shape,
        cost_estimate=pl.CostEstimate(
            flops=3 * rows * depth * width, transcendentals=0,
            bytes_accessed=2 * rows * depth + 4 * width * depth + 2 * rows * width),
        compiler_params=pltpu.CompilerParams(vmem_limit_bytes=LIMIT),
    )(places, ancestor, *operands)


def order_kernel(place_ref, *refs):
    pieces, (one_ref, two_ref) = refs[:8], refs[8:]
    for index, piece_ref in enumerate(pieces):
        size = piece_ref.shape[0] // 2
        span = pl.ds(pl.multiple_of(place_ref[index] * size, size), size)
        one_ref[span, :] = piece_ref[:size, :]
        two_ref[span, :] = piece_ref[size:, :]


def ordered(pieces, places):
    size, depth = pieces[0].shape
    spec = pl.BlockSpec((size, depth), lambda i, places: (0, 0), pipeline_mode=pl.Buffered(1))
    whole = pl.BlockSpec((4 * size, depth), lambda i, places: (0, 0), pipeline_mode=pl.Buffered(1))
    return pl.pallas_call(
        order_kernel,
        grid_spec=pltpu.PrefetchScalarGridSpec(
            num_scalar_prefetch=1, grid=(1,), in_specs=[spec] * 8, out_specs=[whole] * 2),
        out_shape=[jax.ShapeDtypeStruct((4 * size, depth), jnp.float32)] * 2,
        cost_estimate=pl.CostEstimate(flops=0, transcendentals=0, bytes_accessed=64 * size * depth),
        compiler_params=pltpu.CompilerParams(vmem_limit_bytes=40 * 1024 * 1024),
    )(places, *pieces)


def turn_kernel(one_ref, two_ref, one_out, two_out):
    one_out[...] = one_ref[...].T
    two_out[...] = two_ref[...].T


def turned(one, two):
    return pl.pallas_call(
        turn_kernel,
        out_shape=[jax.ShapeDtypeStruct(value.shape[::-1], value.dtype) for value in (one, two)],
        cost_estimate=pl.CostEstimate(flops=0, transcendentals=0, bytes_accessed=16 * one.size),
    )(one, two)


def per_device(ancestor, lhat_one, lhat_two, link_two, diag_one, diag_two, mask_one, mask_two):
    column_index = lax.axis_index(COL)
    core = lax.axis_index("core")
    xl, z = lax.axis_index("xl"), lax.axis_index("z")
    xh, y = lax.axis_index("xh"), lax.axis_index("y")
    rows, depth = ancestor.shape
    width = link_two.shape[0]
    blocks = depth // BLOCK
    strip, half = width // 8, width // 2
    up = [(i, (i + 1) % 4) for i in range(4)]
    down = [(i, (i - 1) % 4) for i in range(4)]

    def places_of(side, ring):
        here = [side * 4 + (ring + step) % 4 for step in range(4)]
        there = [(1 - side) * 4 + (ring + step) % 4 for step in range(4)]
        return [here[0], there[0], here[3], here[1], there[3], there[1], here[2], there[2]]

    row_places = places_of(xl, z)
    own_places = jnp.stack([core] + row_places).astype(jnp.int32)
    other_places = jnp.stack([1 - core] + row_places).astype(jnp.int32)
    plane_places = jnp.stack(places_of(xh, y - z + 4)).astype(jnp.int32)

    def masked(shard, mask):
        own = lax.dynamic_slice_in_dim(mask, column_index * blocks, blocks).astype(jnp.float32)
        return shard.T * jnp.broadcast_to(own[:, None], (blocks, BLOCK)).reshape(1, depth)

    def gathered(piece, side_axis, ring_axis, far_aside=False):
        below = lax.ppermute(piece, ring_axis, up)
        above = lax.ppermute(piece, ring_axis, down)
        side = lax.ppermute(piece, side_axis, SWAP)
        side_below = lax.ppermute(side, ring_axis, up)
        side_above = lax.ppermute(side, ring_axis, down)
        if far_aside:
            middle = piece.shape[0] // 2
            far = jnp.concatenate([lax.ppermute(below[:middle], ring_axis, up),
                                   lax.ppermute(above[middle:], ring_axis, down)])
            side_far = lax.ppermute(far, side_axis, SWAP)
        else:
            far = lax.ppermute(below, ring_axis, up)
            side_far = lax.ppermute(side_above, ring_axis, down)
        return [piece, side, below, above, side_below, side_above, far, side_far]

    def scattered(chip):
        pieces = lax.all_to_all(chip.reshape(8, strip, rows // 2), PLANE,
                                split_axis=0, concat_axis=0, tiled=True)
        return -pieces.sum(0)

    def halves(value, axis):
        size = value.shape[axis] // 2
        cut = lambda side: lax.dynamic_slice_in_dim(value, side * size, size, axis)
        return cut(core), cut(1 - core)

    def to_rows(part_t):
        keep, send = halves(part_t, 0)
        received = lax.ppermute(send, "core", SWAP)
        full = jnp.where(core == 0, jnp.concatenate([keep, received], 1),
                         jnp.concatenate([received, keep], 1))
        return full.T

    def strips(left, right):
        return product(left, right, ((1,), (1,)))

    piece_one = masked(lhat_one, mask_one)
    piece_two = masked(lhat_two, mask_two)
    pieces_one = gathered(piece_one, "xl", "z")
    raw = lax.ppermute(jnp.concatenate([piece_one, piece_two]), ALL, raw_routes())
    row_pieces = gathered(raw, "xh", "y", far_aside=True)
    link_base = lax.optimization_barrier(-product(diag_one, link_two))
    piece_two, *pieces_one = lax.optimization_barrier((piece_two, *pieces_one))
    pieces_two = gathered(piece_two, "xl", "z")

    send_one, *parts_one, factor_one = half_product(ancestor, other_places, pieces_one, kept=True)
    received_one = lax.ppermute(send_one, "core", SWAP)
    (chip_one,) = half_product(ancestor, own_places, parts=parts_one, added=received_one)
    x_one = scattered(chip_one)
    mixed = product(link_two, factor_one, ((0,), (0,)))
    send_two, *parts_two = half_product(ancestor, other_places, pieces_two, minus=mixed)
    received_two = lax.ppermute(send_two, "core", SWAP)
    (chip_two,) = half_product(ancestor, own_places, parts=parts_two, added=received_two)
    x_two = scattered(chip_two)

    rows_one, rows_two = ordered(row_pieces, plane_places)
    parts = jnp.stack([strips(x_one, rows_one), strips(x_one, rows_two), strips(x_two, rows_two)])
    keep, send = halves(parts, 2)
    chip = keep + lax.ppermute(send, "core", SWAP)
    chip = chip.reshape(3, 8, strip // 8, half).transpose(1, 0, 2, 3)
    piece = lax.all_to_all(chip, ROW, split_axis=0, concat_axis=0, tiled=True).sum(0)
    spread = lax.all_to_all(jnp.broadcast_to(piece[None], (64,) + piece.shape), CHIPS,
                            split_axis=0, concat_axis=0, tiled=True)
    spread = spread.reshape(8, 8, 3, strip // 8, half).transpose(2, 1, 0, 3, 4).reshape(3, width, half)
    other = lax.ppermute(spread, "core", SWAP)
    sums = jnp.where(core == 0, jnp.concatenate([spread, other], 2), jnp.concatenate([other, spread], 2))
    one_base, two_base = turned(diag_one, diag_two)
    d_one = (one_base - sums[0]).T
    link_inverse = link_base - sums[1] + product(sums[0], link_two, ((0,), (0,)))
    d_two = (two_base - sums[2] - product(link_inverse, link_two, ((0,), (0,)))).T
    return (to_rows(x_one), d_one, to_rows(x_two), link_inverse, d_two)


def solution(mesh):
    fine = Mesh(mesh.devices.reshape(SIZES), ALL)
    in_specs = (P(ROW, COL), P(COL, ROW), P(COL, ROW), P(), P(), P(), P(), P())
    out_specs = (P(ROW, COL), P(), P(ROW, COL), P(), P())
    return jax.shard_map(
        per_device, mesh=fine, in_specs=in_specs, out_specs=out_specs, check_vma=False
    )
```

```python
import functools

import jax
import jax.numpy as jnp
from jax import lax
from jax.experimental import pallas as pl
from jax.experimental.pallas import tpu as pltpu
from jax.sharding import Mesh, PartitionSpec as P


BLOCK = 128
LIMIT = 32 * 1024 * 1024
ROW = ("xl", "z")
COL = ("xh", "y", "core")
PLANE = ("xh", "y")
CHIPS = ("xl", "z", "xh", "y")
ALL = ROW + COL
SIZES = (2, 4, 2, 4, 2)
SWAP = ((0, 1), (1, 0))


def product(left, right, contract=((1,), (0,))):
    return lax.dot_general(left, right, (contract, ((), ())), precision=lax.Precision.HIGH,
                           preferred_element_type=jnp.float32)


def linear(xl, z, xh, y, core):
    return (((xl * 4 + z) * 2 + xh) * 4 + y) * 2 + core


def raw_routes():
    routes = []
    for xl in range(2):
        for z in range(4):
            for xh in range(2):
                for y in range(4):
                    for core in range(2):
                        source = linear(xh, (y - z) % 4, xl, z, core)
                        routes.append((source, linear(xl, z, xh, y, core)))
    return routes


def split(value):
    high = value.astype(jnp.bfloat16)
    return high, (value - high.astype(jnp.float32)).astype(jnp.bfloat16)


def multiply(a_ref, high_ref, low_ref):
    a_high, a_low = split(a_ref[...])
    dims = (((1,), (1,)), ((), ()))
    dot = lambda l, r: lax.dot_general(l, r, dims, preferred_element_type=jnp.float32)
    return dot(high_ref[...], a_high) + dot(low_ref[...], a_high) + dot(high_ref[...], a_low)


def first_kernel(minus, kept, place_ref, a_ref, *refs):
    refs = list(refs)
    pieces = [refs.pop(0) for _ in range(8)]
    minus_ref = refs.pop(0) if minus else None
    out_ref, high_ref, low_ref = refs[:3]
    factor_ref = refs[3] if kept else None

    @pl.when(pl.program_id(0) == 0)
    def _():
        for index, piece_ref in enumerate(pieces):
            size = piece_ref.shape[0]
            span = pl.ds(pl.multiple_of(place_ref[1 + index] * size, size), size)
            value = piece_ref[...]
            if minus:
                value = value - minus_ref[span, :]
            high, low = split(value)
            if kept:
                factor_ref[span, :] = value
            high_ref[span, :] = high
            low_ref[span, :] = low

    out_ref[...] = multiply(a_ref, high_ref, low_ref)


def second_kernel(place_ref, a_ref, high_ref, low_ref, added_ref, out_ref):
    del place_ref
    out_ref[...] = multiply(a_ref, high_ref, low_ref) + added_ref[...]


def half_product(ancestor, places, pieces=None, minus=None, kept=False, parts=None, added=None):
    rows, depth = ancestor.shape
    width = 8 * pieces[0].shape[0] if pieces else parts[0].shape[0]
    tile = rows // 12
    once = dict(pipeline_mode=pl.Buffered(1))
    whole = pl.BlockSpec((width, depth), lambda i, places: (0, 0), **once)
    piece = pl.BlockSpec((width // 8, depth), lambda i, places: (0, 0), **once)
    column = pl.BlockSpec((width, tile), lambda i, places: (0, i))
    in_specs = [pl.BlockSpec((tile, depth), lambda i, places: (places[0] * 6 + i, 0))]
    out_shape, out_specs = [jax.ShapeDtypeStruct((width, rows // 2), jnp.float32)], [column]
    if pieces:
        kernel = functools.partial(first_kernel, minus is not None, kept)
        operands = [*pieces] + ([] if minus is None else [minus])
        in_specs += [piece] * 8 + ([] if minus is None else [whole])
        for kind in [jnp.bfloat16, jnp.bfloat16] + [jnp.float32] * kept:
            out_shape.append(jax.ShapeDtypeStruct((width, depth), kind))
            out_specs.append(whole)
    else:
        kernel = second_kernel
        operands = [*parts, added]
        in_specs += [whole, whole, column]
    return pl.pallas_call(
        kernel,
        grid_spec=pltpu.PrefetchScalarGridSpec(
            num_scalar_prefetch=1, grid=(6,), in_specs=in_specs, out_specs=out_specs),
        out_shape=out_shape,
        cost_estimate=pl.CostEstimate(
            flops=3 * rows * depth * width, transcendentals=0,
            bytes_accessed=2 * rows * depth + 4 * width * depth + 2 * rows * width),
        compiler_params=pltpu.CompilerParams(vmem_limit_bytes=LIMIT),
    )(places, ancestor, *operands)


def order_kernel(place_ref, *refs):
    pieces, (one_ref, two_ref) = refs[:8], refs[8:]
    for index, piece_ref in enumerate(pieces):
        size = piece_ref.shape[0] // 2
        span = pl.ds(pl.multiple_of(place_ref[index] * size, size), size)
        one_ref[span, :] = piece_ref[:size, :]
        two_ref[span, :] = piece_ref[size:, :]


def ordered(pieces, places):
    size, depth = pieces[0].shape
    spec = pl.BlockSpec((size, depth), lambda i, places: (0, 0), pipeline_mode=pl.Buffered(1))
    whole = pl.BlockSpec((4 * size, depth), lambda i, places: (0, 0), pipeline_mode=pl.Buffered(1))
    return pl.pallas_call(
        order_kernel,
        grid_spec=pltpu.PrefetchScalarGridSpec(
            num_scalar_prefetch=1, grid=(1,), in_specs=[spec] * 8, out_specs=[whole] * 2),
        out_shape=[jax.ShapeDtypeStruct((4 * size, depth), jnp.float32)] * 2,
        cost_estimate=pl.CostEstimate(flops=0, transcendentals=0, bytes_accessed=64 * size * depth),
        compiler_params=pltpu.CompilerParams(vmem_limit_bytes=40 * 1024 * 1024),
    )(places, *pieces)


def turn_kernel(one_ref, two_ref, one_out, two_out):
    one_out[...] = one_ref[...].T
    two_out[...] = two_ref[...].T


def turned(one, two):
    return pl.pallas_call(
        turn_kernel,
        out_shape=[jax.ShapeDtypeStruct(value.shape[::-1], value.dtype) for value in (one, two)],
        cost_estimate=pl.CostEstimate(flops=0, transcendentals=0, bytes_accessed=16 * one.size),
    )(one, two)


def per_device(ancestor, lhat_one, lhat_two, link_two, diag_one, diag_two, mask_one, mask_two):
    column_index = lax.axis_index(COL)
    core = lax.axis_index("core")
    xl, z = lax.axis_index("xl"), lax.axis_index("z")
    xh, y = lax.axis_index("xh"), lax.axis_index("y")
    rows, depth = ancestor.shape
    width = link_two.shape[0]
    blocks = depth // BLOCK
    strip, half = width // 8, width // 2
    up = [(i, (i + 1) % 4) for i in range(4)]
    down = [(i, (i - 1) % 4) for i in range(4)]

    def places_of(side, ring):
        here = [side * 4 + (ring + step) % 4 for step in range(4)]
        there = [(1 - side) * 4 + (ring + step) % 4 for step in range(4)]
        return [here[0], there[0], here[3], here[1], there[3], there[1], here[2], there[2]]

    row_places = places_of(xl, z)
    own_places = jnp.stack([core] + row_places).astype(jnp.int32)
    other_places = jnp.stack([1 - core] + row_places).astype(jnp.int32)
    plane_places = jnp.stack(places_of(xh, y - z + 4)).astype(jnp.int32)

    def masked(shard, mask):
        own = lax.dynamic_slice_in_dim(mask, column_index * blocks, blocks).astype(jnp.float32)
        return shard.T * jnp.broadcast_to(own[:, None], (blocks, BLOCK)).reshape(1, depth)

    def gathered(piece, side_axis, ring_axis):
        below = lax.ppermute(piece, ring_axis, up)
        above = lax.ppermute(piece, ring_axis, down)
        side = lax.ppermute(piece, side_axis, SWAP)
        side_below = lax.ppermute(side, ring_axis, up)
        side_above = lax.ppermute(side, ring_axis, down)
        far = lax.ppermute(below, ring_axis, up)
        side_far = lax.ppermute(side_above, ring_axis, down)
        return [piece, side, below, above, side_below, side_above, far, side_far]

    def scattered(chip):
        pieces = lax.all_to_all(chip.reshape(8, strip, rows // 2), PLANE,
                                split_axis=0, concat_axis=0, tiled=True)
        return -pieces.sum(0)

    def halves(value, axis):
        size = value.shape[axis] // 2
        cut = lambda side: lax.dynamic_slice_in_dim(value, side * size, size, axis)
        return cut(core), cut(1 - core)

    def to_rows(part_t):
        keep, send = halves(part_t, 0)
        received = lax.ppermute(send, "core", SWAP)
        full = jnp.where(core == 0, jnp.concatenate([keep, received], 1),
                         jnp.concatenate([received, keep], 1))
        return full.T

    def strips(left, right):
        return product(left, right, ((1,), (1,)))

    piece_one = masked(lhat_one, mask_one)
    piece_two = masked(lhat_two, mask_two)
    pieces_one = gathered(piece_one, "xl", "z")
    raw = lax.ppermute(jnp.concatenate([piece_one, piece_two]), ALL, raw_routes())
    row_pieces = gathered(raw, "xh", "y")
    link_base = lax.optimization_barrier(-product(diag_one, link_two))
    piece_two, *pieces_one = lax.optimization_barrier((piece_two, *pieces_one))
    pieces_two = gathered(piece_two, "xl", "z")

    send_one, *parts_one, factor_one = half_product(ancestor, other_places, pieces_one, kept=True)
    received_one = lax.ppermute(send_one, "core", SWAP)
    (chip_one,) = half_product(ancestor, own_places, parts=parts_one, added=received_one)
    x_one = scattered(chip_one)
    mixed = product(link_two, factor_one, ((0,), (0,)))
    send_two, *parts_two = half_product(ancestor, other_places, pieces_two, minus=mixed)
    received_two = lax.ppermute(send_two, "core", SWAP)
    (chip_two,) = half_product(ancestor, own_places, parts=parts_two, added=received_two)
    x_two = scattered(chip_two)

    rows_one, rows_two = ordered(row_pieces, plane_places)
    parts = jnp.stack([strips(x_one, rows_one), strips(x_one, rows_two), strips(x_two, rows_two)])
    keep, send = halves(parts, 2)
    chip = keep + lax.ppermute(send, "core", SWAP)
    chip = chip.reshape(3, 8, strip // 8, half).transpose(1, 0, 2, 3)
    piece = lax.all_to_all(chip, ROW, split_axis=0, concat_axis=0, tiled=True).sum(0)
    spread = lax.all_to_all(jnp.broadcast_to(piece[None], (64,) + piece.shape), CHIPS,
                            split_axis=0, concat_axis=0, tiled=True)
    spread = spread.reshape(8, 8, 3, strip // 8, half).transpose(2, 1, 0, 3, 4).reshape(3, width, half)
    other = lax.ppermute(spread, "core", SWAP)
    sums = jnp.where(core == 0, jnp.concatenate([spread, other], 2), jnp.concatenate([other, spread], 2))
    one_base, two_base = turned(diag_one, diag_two)
    d_one = (one_base - sums[0]).T
    link_inverse = link_base - sums[1] + product(sums[0], link_two, ((0,), (0,)))
    d_two = (two_base - sums[2] - product(link_inverse, link_two, ((0,), (0,)))).T
    return (to_rows(x_one), d_one, to_rows(x_two), link_inverse, d_two)


def solution(mesh):
    fine = Mesh(mesh.devices.reshape(SIZES), ALL)
    in_specs = (P(ROW, COL), P(COL, ROW), P(COL, ROW), P(), P(), P(), P(), P())
    out_specs = (P(ROW, COL), P(), P(ROW, COL), P(), P())
    return jax.shard_map(
        per_device, mesh=fine, in_specs=in_specs, out_specs=out_specs, check_vma=False
    )
```
